768 devices in a mesh: gx: 24 (over y, z_hi), gy: 16 (over z_lo, x), gz: 2 (over core).
Axes of the slice: x: 4, y: 8, z: 12 (z_hi: 3, z_lo: 4; z = z_hi * 4 + z_lo), core: 2. Of those that a mesh axis runs over, the one named last changes fastest.
Arguments:
- layer_east: float32 [16, 2048, 3072], P('gz', 'gy', 'gx'), may hold values from -6 to 6
- layer_north: float32 [16, 2048, 3072], P('gz', 'gy', 'gx'), may hold values from -6 to 6
- layer_press: float32 [16, 2048, 3072], P('gz', 'gy', 'gx'), may hold values from -6 to 6
- surface: float32 [2048, 3072], P('gy', 'gx'), may hold values from -3 to 3
- land_sea: int32 [2048, 3072], P('gy', 'gx'), may hold values 0 or 1
- bottom_level: int32 [2048, 3072], P('gy', 'gx'), may hold values from 12 to 16
- coriolis: float32 [2048, 3072], P('gy', 'gx'), may hold values from -1 to 1
- level_thick: float32 [16], P('gz'), may hold values from 0.25 to 0.3
Outputs:
- surface_next: float32 [2048, 3072], P('gy', 'gx')
- east_next: float32 [16, 2048, 3072], P('gz', 'gy', 'gx')
- north_next: float32 [16, 2048, 3072], P('gz', 'gy', 'gx')
The draws below stay inside these ranges and needn't reach their ends.
All inputs are finite; a program needn't handle non-finite values. No bound on the sum of `land_sea` on one device may be relied on, other than what follows from the above.
Results may differ from the reference program's by a relative error of at most 0.00002.
Values sent between devices are 32-bit elements; how exact they have to be, the bound alone decides.
A program may use at most 32 MiB of HBM per device.

```python
import math
import jax
import jax.numpy as jnp

SUBSTEPS = 4
NX = 3072
NY = 2048
K = 16


def plant(result, rng, low, top_value):
    spot = [jax.random.randint(jax.random.fold_in(rng, axis), (), 0, length) for axis, length in enumerate(result.shape)]
    main_axis = result.shape.index(max(result.shape))
    next_to = spot[:main_axis] + [(spot[main_axis] + 1) % result.shape[main_axis]] + spot[main_axis + 1:]
    return result.at[tuple(spot)].set(low).at[tuple(next_to)].set(top_value)


def block_scale(key, dims, split, least, high):
    def one(axis_at, blocks):
        steps = jax.random.uniform(jax.random.fold_in(jax.random.fold_in(key, 6), axis_at), (blocks,), jnp.float32, least / len(split), high / len(split))
        return jnp.repeat(jnp.exp(steps), dims[axis_at] // blocks).reshape((-1,) + (1,) * (len(dims) - axis_at - 1))

    gain = one(*split[0])
    for cut in split[1:]:
        gain = gain * one(*cut)
    return gain


def scatter_about(rng, shape, width, reach, shards=(), kind=jnp.bfloat16):
    drawn = width * jax.random.normal(rng, shape, jnp.float32)
    if shards:
        drawn = drawn * block_scale(rng, shape, shards, -0.22, 0.18)
    return jnp.clip(drawn, -reach, reach).astype(kind)


def setup_inputs(seed: int = 0) -> dict:
    seeds = jax.random.split(jax.random.key(seed), 9)
    return {
        "layer_east": scatter_about(seeds[0], (K, NY, NX), 1.0, 6.0, ((0, 2), (1, 16), (2, 24)), jnp.float32),
        "layer_north": scatter_about(seeds[1], (K, NY, NX), 1.0, 6.0, ((0, 2), (1, 16), (2, 24)), jnp.float32),
        "layer_press": scatter_about(seeds[2], (K, NY, NX), 1.0, 6.0, ((0, 2), (1, 16), (2, 24)), jnp.float32),
        "surface": scatter_about(seeds[3], (NY, NX), 0.5, 3.0, ((0, 16), (1, 24)), jnp.float32),
        "land_sea": plant((jax.random.randint(seeds[4], (NY, NX), 0, 8) < 7).astype(jnp.int32), jax.random.fold_in(seeds[4], 1), 0, 1),
        "bottom_level": plant(jax.random.randint(seeds[5], (NY, NX), K - K // 4, K + 1), jax.random.fold_in(seeds[5], 1), K - K // 4, K).astype(jnp.int32),
        "coriolis": jnp.clip(jax.random.uniform(seeds[6], (NY, NX), jnp.float32, -1.0, 1.0) * block_scale(seeds[6], (NY, NX), ((0, 16), (1, 24)), -0.4, 0.0), -1.0, 1.0),
        "level_thick": jnp.clip(jnp.exp(math.log(0.3) - 0.1823216 * jax.random.uniform(seeds[7], (K,), jnp.float32) ** block_scale(seeds[7], (K,), ((0, 2),), -0.2, 0.2)), 0.25, 0.3),
    }


COURANT = 0.25
VISCOSITY = 0.1


def shifted(field, step, axis):
    return jnp.roll(field, -step, axis=axis)


def layer_terms(centre, east, west, north, south, coriolis):
    vel_east, vel_north, press, active = centre
    grad_x = 0.5 * (east[3] * (east[2] - press) + west[3] * (press - west[2]))
    grad_y = 0.5 * (north[3] * (north[2] - press) + south[3] * (press - south[2]))

    def friction(slot, value):
        return (east[3] * (east[slot] - value) + west[3] * (west[slot] - value)
                + north[3] * (north[slot] - value) + south[3] * (south[slot] - value))

    tend_east = active * (-grad_x + coriolis * vel_north + VISCOSITY * friction(0, vel_east))
    tend_north = active * (-grad_y - coriolis * vel_east + VISCOSITY * friction(1, vel_north))
    return tend_east, tend_north


def surface_step(height, trans_east, trans_north, ocean_mid, depth, coriolis, force_east, force_north):
    spread = 0.5 * (trans_east[1:-1, 2:] - trans_east[1:-1, :-2]) + 0.5 * (trans_north[2:, 1:-1] - trans_north[:-2, 1:-1])
    height_mid = ocean_mid * (height[1:-1, 1:-1] - COURANT * spread)
    slope_x = 0.5 * (height_mid[1:-1, 2:] - height_mid[1:-1, :-2])
    slope_y = 0.5 * (height_mid[2:, 1:-1] - height_mid[:-2, 1:-1])
    ocean_core = ocean_mid[1:-1, 1:-1]
    old_east = trans_east[2:-2, 2:-2]
    old_north = trans_north[2:-2, 2:-2]
    new_east = ocean_core * (old_east + COURANT * (-depth * slope_x + coriolis * old_north + force_east))
    new_north = ocean_core * (old_north + COURANT * (-depth * slope_y - coriolis * old_east + force_north))
    return height_mid, new_east, new_north


def reference(layer_east, layer_north, layer_press, surface, land_sea, bottom_level, coriolis, level_thick):
    levels = layer_east.shape[0]
    ocean = land_sea.astype(jnp.float32)
    deepest = ocean * bottom_level.astype(jnp.float32)
    indices = jnp.arange(levels).astype(jnp.float32)[:, None, None]
    active = (indices < deepest[None]).astype(jnp.float32)
    centre = (layer_east, layer_north, layer_press, active)
    east = tuple(shifted(item, 1, 2) for item in centre)
    west = tuple(shifted(item, -1, 2) for item in centre)
    north = tuple(shifted(item, 1, 1) for item in centre)
    south = tuple(shifted(item, -1, 1) for item in centre)
    tend_east, tend_north = layer_terms(centre, east, west, north, south, coriolis)
    thick = level_thick[:, None, None]
    masked_east = active * layer_east
    masked_north = active * layer_north
    force_east = jnp.sum(thick * tend_east, axis=0)
    force_north = jnp.sum(thick * tend_north, axis=0)
    sum_east = jnp.sum(thick * masked_east, axis=0)
    sum_north = jnp.sum(thick * masked_north, axis=0)
    depth = jnp.sum(thick * active, axis=0)
    height, trans_east, trans_north = surface, sum_east, sum_north
    ocean_wide = jnp.pad(ocean, 1, mode="wrap")
    for step in range(SUBSTEPS):
        height_mid, trans_east, trans_north = surface_step(
            jnp.pad(height, 2, mode="wrap"), jnp.pad(trans_east, 2, mode="wrap"),
            jnp.pad(trans_north, 2, mode="wrap"), ocean_wide, depth, coriolis, force_east, force_north)
        height = height_mid[1:-1, 1:-1]
    timestep = SUBSTEPS * COURANT
    floor_depth = depth + (1.0 - ocean)
    east_next = active * (masked_east + timestep * tend_east + (trans_east - sum_east - timestep * force_east) / floor_depth)
    north_next = active * (masked_north + timestep * tend_north + (trans_north - sum_north - timestep * force_north) / floor_depth)
    return height, east_next, north_next
```

```python
import functools

import jax
import jax.numpy as jnp
from jax import lax
from jax.experimental import pallas as pl
from jax.experimental.pallas import tpu as pltpu
from jax.sharding import PartitionSpec as P

MESH = pl.DeviceIdType.MESH
SUBSTEPS = 4
COURANT = 0.25
VISCOSITY = 0.1
TIMESTEP = SUBSTEPS * COURANT

N = 128
LEVELS = 8
PITCH = 144
PAD = 8
TOP = 16
EXT = 160

HEIGHT, CORIOLIS, DEEPEST, EAST, NORTH, F_EAST, F_NORTH, DEPTH, OCEAN = range(9)
TURNED = (1, 0, 3, 2)


def shift_east(main, side, lane):
    a, b = pltpu.roll(main, N - 1, 1), pltpu.roll(side, N - 1, 1)
    last = lane == N - 1
    return jnp.where(last, b, a), jnp.where(last, a, b)


def shift_west(main, side, lane):
    a, b = pltpu.roll(main, 1, 1), pltpu.roll(side, 1, 1)
    first = lane == 0
    return jnp.where(first, b, a), jnp.where(first, a, b)


def lanes(rows):
    return lax.broadcasted_iota(jnp.int32, (rows, N), 1)


def kernel(
    thick, east_h, north_h, press_h, surf_h, land_h, bottom_h, cor_h,
    base_e, base_n, corr, height_out,
    levels_e, levels_n, levels_p, deep, surf, cor, land, bottom,
    edges, part, part_in, swap, swap_in, late, late_in, totals,
    send1, send2, send_d1, send_d2, recv1, recv2, recv_d1, recv_d2,
    xm, xs, load_sem, send_sem, recv_sem,
):
    gx, gy, gz = lax.axis_index("gx"), lax.axis_index("gy"), lax.axis_index("gz")
    nx, ny = lax.axis_size("gx"), lax.axis_size("gy")
    east, west = lax.rem(gx + 1, nx), lax.rem(gx + nx - 1, nx)
    north, south = lax.rem(gy + 1, ny), lax.rem(gy + ny - 1, ny)
    sister = {"gz": 1 - gz}
    straight = ({"gx": east}, {"gx": west}, {"gy": north}, {"gy": south})
    diagonal = (
        {"gx": east, "gy": north}, {"gx": west, "gy": north},
        {"gx": east, "gy": south}, {"gx": west, "gy": south},
    )

    barrier = pltpu.get_barrier_semaphore()
    for other in (*diagonal, *straight, sister):
        pl.semaphore_signal(barrier, inc=1, device_id=other, device_id_type=MESH)

    loads = []

    def load(source, target):
        copy = pltpu.make_async_copy(source, target, load_sem.at[len(loads)])
        copy.start()
        loads.append(copy)

    load(land_h, land)
    load(bottom_h, bottom)
    load(surf_h, surf)
    load(cor_h, cor)
    levels = (levels_e, levels_n, levels_p)
    for k in range(LEVELS):
        for source, target in zip((east_h, north_h, press_h), levels):
            load(source.at[pl.ds(k * N, N)], target.at[pl.ds(k * PITCH + PAD, N)])

    lane = lanes(8)
    even = (lane & 1) == 0
    left_half = lane < 64
    row = lax.broadcasted_iota(jnp.int32, (8, N), 0)
    first_level = (gz * LEVELS).astype(jnp.float32)
    zero = jnp.zeros((8, N), jnp.float32)

    def by_index(index):
        out = zero
        for k in range(LEVELS):
            out = jnp.where(index == k, thick[k], out)
        return out

    for k in range(4):
        loads[k].wait()
    deep[0:PAD, :] = zero
    deep[PAD + N : PITCH, :] = zero
    deep[PAD : PAD + N, :] = land[...].astype(jnp.float32) * bottom[...].astype(jnp.float32)
    for copy in loads[4:]:
        copy.wait()

    def chunk(i, carry):
        rows = 16
        at = pl.multiple_of(i * rows, rows)
        lane16 = lanes(rows)
        d = deep[pl.ds(at + PAD, rows), :]
        d_e = jnp.where(lane16 == N - 1, 0.0, pltpu.roll(d, N - 1, 1))
        d_w = jnp.where(lane16 == 0, 0.0, pltpu.roll(d, 1, 1))
        d_n = deep[pl.ds(at + PAD + 1, rows), :]
        d_s = deep[pl.ds(at + PAD - 1, rows), :]
        f = cor[pl.ds(at, rows), :]
        sums = [jnp.zeros((rows, N), jnp.float32) for _ in range(4)]
        for k in range(LEVELS):
            level = first_level + k
            here = level < d
            on_e, on_w, on_n, on_s = (level < other for other in (d_e, d_w, d_n, d_s))
            start = k * PITCH + PAD + at

            def around(ref):
                c = ref[pl.ds(start, rows), :]
                e = jnp.where(on_e, pltpu.roll(c, N - 1, 1) - c, 0.0)
                w = jnp.where(on_w, pltpu.roll(c, 1, 1) - c, 0.0)
                n = jnp.where(on_n, ref[pl.ds(start + 1, rows), :] - c, 0.0)
                s = jnp.where(on_s, ref[pl.ds(start - 1, rows), :] - c, 0.0)
                return c, e, w, n, s

            ve, e_e, e_w, e_n, e_s = around(levels_e)
            vn, n_e, n_w, n_n, n_s = around(levels_n)
            _, p_e, p_w, p_n, p_s = around(levels_p)
            tend_e = jnp.where(
                here, 0.5 * (p_w - p_e) + f * vn + VISCOSITY * ((e_e + e_w) + (e_n + e_s)), 0.0
            )
            tend_n = jnp.where(
                here, 0.5 * (p_s - p_n) - f * ve + VISCOSITY * ((n_e + n_w) + (n_n + n_s)), 0.0
            )
            masked_e = jnp.where(here, ve, 0.0)
            masked_n = jnp.where(here, vn, 0.0)
            base_e[pl.ds(k * N + at, rows), :] = masked_e + TIMESTEP * tend_e
            base_n[pl.ds(k * N + at, rows), :] = masked_n + TIMESTEP * tend_n
            weight = thick[k]
            for slot, value in enumerate((masked_e, masked_n, tend_e, tend_n)):
                sums[slot] += weight * value
        for slot in range(4):
            part[slot, pl.ds(at, rows), :] = sums[slot]
        return carry

    lax.fori_loop(0, N // 16, chunk, 0)

    def pack(g, carry):
        carry = list(carry)
        to_east = (lane >> 3) == g
        to_west = (lane >> 3) == lax.rem(g + 1, 16)
        at = pl.multiple_of(g * 8, 8)
        turn = lax.rem(8 * g + 8, N)
        fields = [part.at[slot] for slot in range(4)] + [surf, cor]
        for i, ref in enumerate(fields):
            v = pltpu.roll(ref[pl.ds(at, 8), :], turn, 1)
            carry[i] = jnp.where(to_east, v, carry[i])
            carry[7 + i] = jnp.where(to_west, v, carry[7 + i])
        d = deep[pl.ds(at + PAD, 8), :]
        v = pltpu.roll(d, turn, 1)
        carry[6] = jnp.where(to_east, v, carry[6])
        carry[13] = jnp.where(to_west, v, carry[13])
        pair = (lane - 8 * g) >> 1
        carry[14] = jnp.where(pair == 0, pltpu.roll(d, 8 * g + 1, 1), carry[14])
        for t, ref in enumerate(levels):
            for k in range(LEVELS):
                v = pltpu.roll(ref[pl.ds(at + (k * PITCH + PAD), 8), :], 8 * g + 2 * (k % 4) + 1, 1)
                slot = 15 + 2 * t + k // 4
                carry[slot] = jnp.where(pair == k % 4, v, carry[slot])
        return tuple(carry)

    packed = lax.fori_loop(0, 16, pack, (zero,) * 21)
    to_e, to_w, d_edge, edge = packed[0:7], packed[7:14], packed[14], packed[15:21]
    d_edge = d_edge + pltpu.roll(d_edge, 2, 1)
    d_edge = d_edge + pltpu.roll(d_edge, 4, 1)
    for j in range(6):
        edges[j] = edge[j]
    edges[6] = d_edge
    row_n = [ref[pl.ds(PAD + N - 1, LEVELS, stride=PITCH), :] for ref in levels]
    row_s = [ref[pl.ds(PAD, LEVELS, stride=PITCH), :] for ref in levels]

    def pack_ends(tiles):
        high = low = zero
        for j, v in enumerate(tiles):
            v = pltpu.roll(v, 8 * j + 8, 1)
            high = jnp.where((lane >> 3) == j, v, high)
            low = jnp.where((lane >> 3) == j + 1, v, low)
        return high, low

    rows_e, rows_w = pack_ends([r for t in range(3) for r in (row_n[t], row_s[t])])
    cols_n, cols_s = pack_ends(edge)
    flat = (surf, cor)
    tiles_n = [ref[N - 8 : N, :] for ref in flat] + [deep[PAD + N - 8 : PAD + N, :]]
    tiles_s = [ref[0:8, :] for ref in flat] + [deep[PAD : PAD + 8, :]]
    for i in range(3):
        send1[0, i] = to_e[4 + i]
        send1[1, i] = to_w[4 + i]
        send1[2, i] = tiles_n[i]
        send1[3, i] = tiles_s[i]
    for t in range(3):
        a, b = edge[2 * t], edge[2 * t + 1]
        send1[0, 3 + t] = jnp.where(even, a, pltpu.roll(b, 1, 1))
        send1[1, 3 + t] = jnp.where(even, pltpu.roll(b, N - 1, 1), a)
        send1[2, 3 + t] = row_n[t]
        send1[3, 3 + t] = row_s[t]
    for i, tile in enumerate((rows_e, rows_w, cols_n, cols_s)):
        send1[i, 6] = tile
    corner_n, corner_s = pack_ends(tiles_n), pack_ends(tiles_s)
    for i, tiles in enumerate((
        (rows_e, cols_n, corner_n[0]), (rows_w, cols_n, corner_n[1]),
        (rows_e, cols_s, corner_s[0]), (rows_w, cols_s, corner_s[1]),
    )):
        for j, tile in enumerate(tiles):
            send_d1[i, j] = tile
    for f in range(4):
        swap[f] = to_e[f]
        swap[4 + f] = to_w[f]
        swap[8 + f] = part[f, N - 8 : N, :]
        swap[12 + f] = part[f, 0:8, :]
    swap[16] = by_index(row)

    copies = {}

    def send(name, source, target, slot, other):
        copy = pltpu.make_async_remote_copy(
            src_ref=source, dst_ref=target, send_sem=send_sem.at[slot], recv_sem=recv_sem.at[slot],
            device_id=other, device_id_type=MESH,
        )
        copy.start()
        copies[name] = copy

    pl.semaphore_wait(barrier, 9)
    send("swap", swap, swap_in, 0, sister)
    for i in range(4):
        send(("d1", i), send_d1.at[i], recv_d1.at[3 - i], 3 + i, diagonal[i])
    for i in range(4):
        send(("s1", i), send1.at[i], recv1.at[TURNED[i]], 7 + i, straight[i])
    send("part", part, part_in, 1, sister)

    copies["swap"].wait_recv()
    whole = [swap[j] + swap_in[j] for j in range(16)]
    for i in range(4):
        for f in range(4):
            send2[i, f] = whole[4 * i + f]
    ends_n, ends_s = pack_ends(whole[8:12]), pack_ends(whole[12:16])
    for i, tile in enumerate((*ends_n, *ends_s)):
        send_d2[i] = tile
    for i in range(4):
        send(("d2", i), send_d2.at[i], recv_d2.at[3 - i], 11 + i, diagonal[i])
    for i in range(4):
        send(("s2", i), send2.at[i], recv2.at[TURNED[i]], 15 + i, straight[i])

    upper = gz == 1
    own_thick, other_thick = swap[16], swap_in[16]
    thick_low = jnp.where(upper, other_thick, own_thick)
    thick_high = jnp.where(upper, own_thick, other_thick)

    def depth_of(d):
        out = jnp.zeros_like(d)
        for k in range(2 * LEVELS):
            tile = thick_low if k < LEVELS else thick_high
            weight = jnp.broadcast_to(tile[k % LEVELS : k % LEVELS + 1, :], d.shape)
            out = out + jnp.where(k < d, weight, 0.0)
        return out

    def settle(ref, at, rows):
        d = ref[DEEPEST, pl.ds(at, rows), :]
        ref[DEPTH, pl.ds(at, rows), :] = depth_of(d)
        ref[OCEAN, pl.ds(at, rows), :] = jnp.where(d > 0.0, 1.0, 0.0)

    xm[HEIGHT, TOP : TOP + N, :] = surf[...]
    xm[CORIOLIS, TOP : TOP + N, :] = cor[...]
    xm[DEEPEST, TOP : TOP + N, :] = deep[PAD : PAD + N, :]

    def settle_main(i, carry):
        settle(xm, pl.multiple_of(TOP + 16 * i, 8), 16)
        return carry

    lax.fori_loop(0, N // 16, settle_main, 0)
    copies["part"].wait_recv()
    for f in range(4):
        whole_f = part[f] + part_in[f]
        xm[EAST + f, TOP : TOP + N, :] = whole_f
        if f < 2:
            totals[f] = whole_f

    for i in range(4):
        copies["d1", i].wait_recv()
        copies["s1", i].wait_recv()
    from_e, from_w, from_n, from_s = (recv1.at[i] for i in range(4))

    def beside(tile_e, tile_w, index):
        turn = (N - 8 * (index + 1)) % N if isinstance(index, int) else lax.rem(2 * N - 8 * (index + 1), N)
        return jnp.where(left_half, pltpu.roll(tile_e, turn, 1), pltpu.roll(tile_w, turn, 1))

    for f in range(3):
        xm[f, TOP + N : TOP + N + 8, :] = from_n[f]
        xm[f, TOP - 8 : TOP, :] = from_s[f]
        xs[f, TOP + N : TOP + N + 8, :] = beside(recv_d1[0, 2], recv_d1[1, 2], f)
        xs[f, TOP - 8 : TOP, :] = beside(recv_d1[2, 2], recv_d1[3, 2], f)

    def unpack_inputs(g, carry):
        at = pl.multiple_of(TOP + 8 * g, 8)
        for f in range(3):
            xs[f, pl.ds(at, 8), :] = beside(from_e[f], from_w[f], g)
        return carry

    lax.fori_loop(0, 16, unpack_inputs, 0)

    east_of = lane & 1
    sign = jnp.where(even, -0.5, 0.5)
    in_group = lane & 7

    strip_d = jnp.where(
        in_group == 0, pltpu.roll(from_e[2], N - 8, 1),
        jnp.where(in_group == 1, pltpu.roll(from_w[2], N - 6, 1), 0.0),
    )
    strip_d = strip_d + pltpu.roll(strip_d, 2, 1)
    strip_d = strip_d + pltpu.roll(strip_d, 4, 1)
    own_d = edges[6]
    column_terms = []
    sums_g = sums_e = sums_n = zero
    for half in range(2):
        level_in = (in_group >> 1) + 4 * half
        level = level_in.astype(jnp.float32) + first_level
        both = (level < own_d) & (level < strip_d)
        weight = by_index(level_in)
        diff = []
        for t in range(3):
            if half == 0:
                halo = jnp.where(even, pltpu.roll(from_e[3 + t], N - 1, 1), pltpu.roll(from_w[3 + t], 1, 1))
            else:
                halo = jnp.where(even, from_e[3 + t], from_w[3 + t])
            diff.append(jnp.where(both, halo - edges[2 * t + half], 0.0))
        drag_e, drag_n, grad = VISCOSITY * diff[0], VISCOSITY * diff[1], sign * diff[2]
        column_terms.append((grad + drag_e, drag_n))
        sums_g = sums_g + weight * grad
        sums_e = sums_e + weight * drag_e
        sums_n = sums_n + weight * drag_n

    def over_levels(v):
        v = v + pltpu.roll(v, N - 2, 1)
        return v + pltpu.roll(v, N - 4, 1)

    def swapped(v):
        return jnp.where(even, pltpu.roll(v, N - 1, 1), pltpu.roll(v, 1, 1))

    sums_g, sums_e, sums_n = over_levels(sums_g), over_levels(sums_e), over_levels(sums_n)
    late[0] = jnp.where(
        in_group < 2, sums_g + sums_e,
        jnp.where(
            in_group < 4, pltpu.roll(sums_n, 2, 1),
            jnp.where(
                in_group < 6, pltpu.roll(swapped(sums_g - sums_e), 4, 1), pltpu.roll(swapped(-sums_n), 6, 1)
            ),
        ),
    )

    in_tile = (lane & 15) >> 1
    tile_level = in_tile.astype(jnp.float32) + first_level
    tile_weight = by_index(in_tile) * jnp.where(lane < 32, VISCOSITY, sign)
    for slot, (tile, ahead, behind, corner_at, near, far) in enumerate((
        (from_n[6], recv_d1[0, 1], recv_d1[1, 1], TOP + N, from_n[2], N - 8),
        (from_s[6], recv_d1[2, 1], recv_d1[3, 1], TOP - 8, from_s[2], 0),
    )):
        side = xs[DEEPEST, pl.ds(corner_at, 8), :]

        def ends(v, a, b):
            return jnp.where(
                even, jnp.broadcast_to(v[:, a : a + 1], (8, N)), jnp.broadcast_to(v[:, b : b + 1], (8, N))
            )

        both = (tile_level < ends(near, N - 1, 0)) & (tile_level < ends(side, 0, N - 1))
        halo = jnp.where(even, pltpu.roll(ahead, N - 1, 1), pltpu.roll(behind, 1, 1))
        diff = halo - tile
        if far:
            diff = pltpu.roll(diff, far, 1)
        v = over_levels(jnp.where(both, tile_weight * diff, 0.0))
        late[1 + slot] = v + pltpu.roll(v, N - 8, 1)

    row_level = row.astype(jnp.float32) + first_level
    row_weight = by_index(row)

    def row_pairs(own, halo, d_own, d_halo, factor):
        both = (row_level < d_own) & (row_level < d_halo)
        diff = [jnp.where(both, h - o, 0.0) for h, o in zip(halo, own)]
        return factor * diff[2], VISCOSITY * diff[0], VISCOSITY * diff[1]

    def spread_row(v):
        return jnp.broadcast_to(v, (8, N))

    own_rows_n = [ref[pl.ds(PAD + N - 1, LEVELS, stride=PITCH), :] for ref in levels]
    own_rows_s = [ref[pl.ds(PAD, LEVELS, stride=PITCH), :] for ref in levels]
    main_n = row_pairs(
        own_rows_n, [from_n[3 + t] for t in range(3)],
        spread_row(deep[PAD + N - 1 : PAD + N, :]), spread_row(from_n[2, 0:1, :]), -0.5,
    )
    main_s = row_pairs(
        own_rows_s, [from_s[3 + t] for t in range(3)],
        spread_row(deep[PAD : PAD + 1, :]), spread_row(from_s[2, 7:8, :]), 0.5,
    )
    side_n = row_pairs(
        [beside(from_e[6], from_w[6], 2 * t) for t in range(3)],
        [beside(recv_d1[0, 0], recv_d1[1, 0], 2 * t + 1) for t in range(3)],
        spread_row(xs[DEEPEST, TOP + N - 1 : TOP + N, :]), spread_row(xs[DEEPEST, TOP + N : TOP + N + 1, :]), -0.5,
    )
    side_s = row_pairs(
        [beside(from_e[6], from_w[6], 2 * t + 1) for t in range(3)],
        [beside(recv_d1[2, 0], recv_d1[3, 0], 2 * t) for t in range(3)],
        spread_row(xs[DEEPEST, TOP : TOP + 1, :]), spread_row(xs[DEEPEST, TOP - 1 : TOP, :]), 0.5,
    )
    for slot, pairs in ((3, (main_n, main_s)), (4, (side_n, side_s))):
        tile = zero
        for i, terms in enumerate(pairs):
            for j, term in enumerate(terms):
                total = jnp.sum(row_weight * term, axis=0, keepdims=True)
                tile = jnp.where(row == 3 * i + j, spread_row(total), tile)
        late[slot] = tile
    send("late", late, late_in, 2, sister)

    for at, (grad, drag_e, drag_n) in ((N - 1, main_n), (0, main_s)):
        where_ = pl.ds(at, LEVELS, stride=N)
        base_e[where_, :] = base_e[where_, :] + TIMESTEP * drag_e
        base_n[where_, :] = base_n[where_, :] + TIMESTEP * (grad + drag_n)
    for half in range(2):
        for j in range(2):
            edges[2 * half + j] = TIMESTEP * column_terms[half][j]
    outer = (lane == 0) | (lane == N - 1)

    def add_columns(g, carry):
        for k in range(LEVELS):
            at = pl.multiple_of(g * 8 + k * N, 8)
            turn = (N - 1 - 2 * (k % 4)) - 8 * g
            for j, ref in enumerate((base_e, base_n)):
                v = pltpu.roll(edges[2 * (k // 4) + j], turn, 1)
                ref[pl.ds(at, 8), :] = ref[pl.ds(at, 8), :] + jnp.where(outer, v, 0.0)
        return carry

    lax.fori_loop(0, 16, add_columns, 0)

    def settle_side(i, carry):
        settle(xs, pl.multiple_of(8 + 16 * i, 8), 16)
        return carry

    lax.fori_loop(0, 9, settle_side, 0)
    settle(xm, TOP - 8, 8)
    settle(xm, TOP + N, 8)

    for i in range(4):
        copies["d2", i].wait_recv()
        copies["s2", i].wait_recv()
    for f in range(4):
        xm[EAST + f, TOP + N : TOP + N + 8, :] = recv2[2, f]
        xm[EAST + f, TOP - 8 : TOP, :] = recv2[3, f]
        xs[EAST + f, TOP + N : TOP + N + 8, :] = beside(recv_d2[0], recv_d2[1], f)
        xs[EAST + f, TOP - 8 : TOP, :] = beside(recv_d2[2], recv_d2[3], f)

    copies["late"].wait_recv()
    column_sum = late[0] + late_in[0]

    def unpack_sums(g, carry):
        at = pl.multiple_of(TOP + 8 * g, 8)
        for f in range(2):
            xs[EAST + f, pl.ds(at, 8), :] = beside(recv2[0, f], recv2[1, f], g)
        for f in range(2):
            turn = (N - 1 - 2 * f) - 8 * g
            v = pltpu.roll(column_sum, turn, 1)
            xm[F_EAST + f, pl.ds(at, 8), :] = xm[F_EAST + f, pl.ds(at, 8), :] + jnp.where(outer, v, 0.0)
            v = pltpu.roll(column_sum, turn - 4, 1)
            strip = beside(recv2[0, 2 + f], recv2[1, 2 + f], g)
            xs[F_EAST + f, pl.ds(at, 8), :] = strip + jnp.where(outer, v, 0.0)
        return carry

    lax.fori_loop(0, 16, unpack_sums, 0)

    def add_to(ref, field, at, value):
        ref[field, at, :] = ref[field, at, :] + value

    for slot, at in ((1, pl.ds(TOP + N, 8)), (2, pl.ds(TOP - 8, 8))):
        v = late[slot] + late_in[slot]
        drag_e, drag_n, grad = v, pltpu.roll(v, N - 16, 1), pltpu.roll(v, N - 32, 1)
        add_to(xm, F_EAST, at, jnp.where(outer, pltpu.roll(grad + drag_e, N - 1, 1), 0.0))
        add_to(xm, F_NORTH, at, jnp.where(outer, pltpu.roll(drag_n, N - 1, 1), 0.0))
        add_to(xs, F_EAST, at, jnp.where(outer, pltpu.roll(swapped(grad - drag_e), N - 1, 1), 0.0))
        add_to(xs, F_NORTH, at, jnp.where(outer, pltpu.roll(swapped(-drag_n), N - 1, 1), 0.0))
    for slot, ref in ((3, xm), (4, xs)):
        v = late[slot] + late_in[slot]
        for i, (own, halo) in enumerate(((TOP + N - 1, TOP + N), (TOP, TOP - 1))):
            grad, drag_e, drag_n = (v[3 * i + j : 3 * i + j + 1, :] for j in range(3))
            add_to(ref, F_EAST, pl.ds(own, 1), drag_e)
            add_to(ref, F_NORTH, pl.ds(own, 1), grad + drag_n)
            add_to(ref, F_EAST, pl.ds(halo, 1), -drag_e)
            add_to(ref, F_NORTH, pl.ds(halo, 1), grad - drag_n)

    rows = 48
    lane_r = lanes(rows)
    for step in range(SUBSTEPS):
        for at in range(8, 8 + 3 * rows, rows):
            here = slice(at, at + rows)
            up, down = slice(at + 1, at + rows + 1), slice(at - 1, at + rows - 1)
            main, side = xm[EAST, here, :], xs[EAST, here, :]
            e = shift_east(main, side, lane_r)
            w = shift_west(main, side, lane_r)
            for ref, e_, w_ in ((xm, e[0], w[0]), (xs, e[1], w[1])):
                spread = 0.5 * (e_ - w_) + 0.5 * (ref[NORTH, up, :] - ref[NORTH, down, :])
                ref[HEIGHT, here, :] = ref[OCEAN, here, :] * (ref[HEIGHT, here, :] - COURANT * spread)
        for at in range(8, 8 + 3 * rows, rows):
            here = slice(at, at + rows)
            up, down = slice(at + 1, at + rows + 1), slice(at - 1, at + rows - 1)
            main, side = xm[HEIGHT, here, :], xs[HEIGHT, here, :]
            e = shift_east(main, side, lane_r)
            w = shift_west(main, side, lane_r)
            for ref, e_, w_ in ((xm, e[0], w[0]), (xs, e[1], w[1])):
                if ref is xs and step == SUBSTEPS - 1:
                    continue
                slope_x = 0.5 * (e_ - w_)
                slope_y = 0.5 * (ref[HEIGHT, up, :] - ref[HEIGHT, down, :])
                old_e, old_n = ref[EAST, here, :], ref[NORTH, here, :]
                depth, f, ocean = ref[DEPTH, here, :], ref[CORIOLIS, here, :], ref[OCEAN, here, :]
                ref[EAST, here, :] = ocean * (
                    old_e + COURANT * (-depth * slope_x + f * old_n + ref[F_EAST, here, :])
                )
                ref[NORTH, here, :] = ocean * (
                    old_n + COURANT * (-depth * slope_y - f * old_e + ref[F_NORTH, here, :])
                )

    block = slice(TOP, TOP + N)
    floor_depth = xm[DEPTH, block, :] + (1.0 - xm[OCEAN, block, :])
    for f in range(2):
        corr[f] = (xm[EAST + f, block, :] - totals[f] - TIMESTEP * xm[F_EAST + f, block, :]) / floor_depth
    height_out[...] = xm[HEIGHT, block, :]
    for copy in copies.values():
        copy.wait_send()


def on_device(
    layer_east, layer_north, layer_press, surface, land_sea, bottom_level, coriolis, level_thick
):
    f32 = jnp.float32
    flat = (LEVELS * N, N)
    hbm, vmem = pl.BlockSpec(memory_space=pl.ANY), pl.BlockSpec(memory_space=pltpu.VMEM)
    base_e, base_n, corr, height = pl.pallas_call(
        kernel,
        name="ocean",
        out_shape=(
            jax.ShapeDtypeStruct(flat, f32),
            jax.ShapeDtypeStruct(flat, f32),
            jax.ShapeDtypeStruct((2, N, N), f32),
            jax.ShapeDtypeStruct((N, N), f32),
        ),
        in_specs=[pl.BlockSpec(memory_space=pltpu.SMEM)] + [hbm] * 7,
        out_specs=(vmem,) * 4,
        scratch_shapes=[
            *[pltpu.VMEM((LEVELS * PITCH, N), f32)] * 3,
            pltpu.VMEM((PITCH, N), f32),
            *[pltpu.VMEM((N, N), f32)] * 2,
            *[pltpu.VMEM((N, N), jnp.int32)] * 2,
            pltpu.VMEM((7, 8, N), f32),
            *[pltpu.VMEM((4, N, N), f32)] * 2,
            *[pltpu.VMEM((17, 8, N), f32)] * 2,
            *[pltpu.VMEM((5, 8, N), f32)] * 2,
            pltpu.VMEM((2, N, N), f32),
            *[
                pltpu.VMEM(shape, f32)
                for _ in range(2)
                for shape in ((4, 7, 8, N), (4, 4, 8, N), (4, 3, 8, N), (4, 8, N))
            ],
            *[pltpu.VMEM((9, EXT, N), f32)] * 2,
            pltpu.SemaphoreType.DMA((28,)),
            pltpu.SemaphoreType.DMA((19,)),
            pltpu.SemaphoreType.DMA((19,)),
        ],
        compiler_params=pltpu.CompilerParams(collective_id=0, has_side_effects=True),
    )(
        level_thick,
        layer_east.reshape(flat),
        layer_north.reshape(flat),
        layer_press.reshape(flat),
        surface,
        land_sea,
        bottom_level,
        coriolis,
    )
    deepest = land_sea * bottom_level
    indices = (lax.axis_index("gz") * LEVELS + jnp.arange(LEVELS))[:, None, None]
    active = indices < deepest[None]
    shape = (LEVELS, N, N)
    east_next = jnp.where(active, base_e.reshape(shape) + corr[0], 0.0)
    north_next = jnp.where(active, base_n.reshape(shape) + corr[1], 0.0)
    return height, east_next, north_next


def solution(mesh):
    whole, flat = P("gz", "gy", "gx"), P("gy", "gx")
    return jax.shard_map(
        on_device,
        mesh=mesh,
        in_specs=(whole, whole, whole, flat, flat, flat, flat, P("gz")),
        out_specs=(flat, whole, whole),
        check_vma=False,
    )
```

```python
import jax
import jax.numpy as jnp
from jax import lax
from jax.experimental import pallas as pl
from jax.experimental.pallas import tpu as pltpu
from jax.sharding import PartitionSpec as P

MESH = pl.DeviceIdType.MESH
SUBSTEPS = 4
COURANT = 0.25
VISCOSITY = 0.1
TIMESTEP = SUBSTEPS * COURANT
assert TIMESTEP == 1.0
VMEM_LIMIT = 16 * 2**20

N = 128
LEVELS = 8
PITCH = 144
PAD = 8
TOP = 16
EXT = 160

HEIGHT, CORIOLIS, DEEPEST, EAST, NORTH, F_EAST, F_NORTH, DEPTH, OCEAN = range(9)
TURNED = (1, 0, 3, 2)


def shift_east(main, side, lane):
    a, b = pltpu.roll(main, N - 1, 1), pltpu.roll(side, N - 1, 1)
    last = lane == N - 1
    return jnp.where(last, b, a), jnp.where(last, a, b)


def shift_west(main, side, lane):
    a, b = pltpu.roll(main, 1, 1), pltpu.roll(side, 1, 1)
    first = lane == 0
    return jnp.where(first, b, a), jnp.where(first, a, b)


def lanes(rows):
    return lax.broadcasted_iota(jnp.int32, (rows, N), 1)


def kernel(
    thick_h, east_h, north_h, press_h, surf_h, land_h, bottom_h, cor_h,
    base_e, base_n, corr, height_out, deep_out,
    thick, levels_e, levels_n, levels_p, deep, surf, cor, land, bottom,
    edges, part, part_in, swap, swap_in, late, late_in, totals,
    send1, send2, send_d1, send_d2, recv1, recv2, recv_d1, recv_d2,
    xm, xs, load_sem, send_sem, recv_sem,
):
    gx, gy, gz = lax.axis_index("gx"), lax.axis_index("gy"), lax.axis_index("gz")
    nx, ny = lax.axis_size("gx"), lax.axis_size("gy")
    east, west = lax.rem(gx + 1, nx), lax.rem(gx + nx - 1, nx)
    north, south = lax.rem(gy + 1, ny), lax.rem(gy + ny - 1, ny)
    sister = {"gz": 1 - gz}
    straight = ({"gx": east}, {"gx": west}, {"gy": north}, {"gy": south})
    diagonal = (
        {"gx": east, "gy": north}, {"gx": west, "gy": north},
        {"gx": east, "gy": south}, {"gx": west, "gy": south},
    )

    barrier = pltpu.get_barrier_semaphore()
    for other in (*diagonal, *straight, sister):
        pl.semaphore_signal(barrier, inc=1, device_id=other, device_id_type=MESH)

    loads = []

    def load(source, target):
        copy = pltpu.make_async_copy(source, target, load_sem.at[len(loads)])
        copy.start()
        loads.append(copy)

    load(thick_h, thick)
    load(land_h, land)
    load(bottom_h, bottom)
    load(surf_h, surf)
    load(cor_h, cor)
    levels = (levels_e, levels_n, levels_p)
    for source, target in zip((east_h, north_h, press_h), levels):
        for k in range(LEVELS):
            load(source.at[pl.ds(k * N, N)], target.at[pl.ds(k * PITCH + PAD, N)])

    lane = lanes(8)
    even = (lane & 1) == 0
    left_half = lane < 64
    row = lax.broadcasted_iota(jnp.int32, (8, N), 0)
    first_level = (gz * LEVELS).astype(jnp.float32)
    zero = jnp.zeros((8, N), jnp.float32)

    def by_index(index):
        out = zero
        for k in range(LEVELS):
            out = jnp.where(index == k, thick[k], out)
        return out

    for copy in loads[:5]:
        copy.wait()
    deep[0:PAD, :] = zero
    deep[PAD + N : PITCH, :] = zero
    deepest = land[...].astype(jnp.float32) * bottom[...].astype(jnp.float32)
    deep[PAD : PAD + N, :] = deepest
    deep_out[...] = deepest

    def each_group(body, carry=()):
        def trip(i, carry):
            for u in range(4):
                carry = body(4 * i + u, carry)
            return carry

        return lax.fori_loop(0, 4, trip, carry)

    def strips(refs):
        def body(g, carry):
            to_east = (lane >> 3) == g
            to_west = (lane >> 3) == lax.rem(g + 1, 16)
            turn = lax.rem(8 * g + 8, N)
            out = []
            for i, (ref, pad) in enumerate(refs):
                v = pltpu.roll(ref[pl.ds(pl.multiple_of(g * 8 + pad, 8), 8), :], turn, 1)
                out += [jnp.where(to_east, v, carry[2 * i]), jnp.where(to_west, v, carry[2 * i + 1])]
            return tuple(out)

        tiles = each_group(body, (zero,) * (2 * len(refs)))
        return tiles[0::2], tiles[1::2]

    to_e, to_w = strips([(surf, 0), (cor, 0), (deep, PAD)])

    def pack_deepest(g, d_edge):
        v = pltpu.roll(deep[pl.ds(pl.multiple_of(g * 8 + PAD, 8), 8), :], 8 * g + 1, 1)
        return jnp.where(((lane - 8 * g) >> 1) == 0, v, d_edge)

    d_edge = each_group(pack_deepest, zero)
    d_edge = d_edge + pltpu.roll(d_edge, 2, 1)
    d_edge = d_edge + pltpu.roll(d_edge, 4, 1)
    edges[6] = d_edge

    edge = []
    for t, ref in enumerate(levels):
        for copy in loads[5 + LEVELS * t : 5 + LEVELS * (t + 1)]:
            copy.wait()

        def pack(g, carry, ref=ref):
            carry = list(carry)
            pair = (lane - 8 * g) >> 1
            for k in range(LEVELS):
                at = pl.multiple_of(g * 8 + (k * PITCH + PAD), 8)
                v = pltpu.roll(ref[pl.ds(at, 8), :], 8 * g + 2 * (k % 4) + 1, 1)
                carry[k // 4] = jnp.where(pair == k % 4, v, carry[k // 4])
            return tuple(carry)

        edge += each_group(pack, (zero, zero))
    for j in range(6):
        edges[j] = edge[j]
    row_n = [ref[pl.ds(PAD + N - 1, LEVELS, stride=PITCH), :] for ref in levels]
    row_s = [ref[pl.ds(PAD, LEVELS, stride=PITCH), :] for ref in levels]

    def pack_ends(tiles):
        high = low = zero
        for j, v in enumerate(tiles):
            v = pltpu.roll(v, 8 * j + 8, 1)
            high = jnp.where((lane >> 3) == j, v, high)
            low = jnp.where((lane >> 3) == j + 1, v, low)
        return high, low

    rows_e, rows_w = pack_ends([r for t in range(3) for r in (row_n[t], row_s[t])])
    cols_n, cols_s = pack_ends(edge)
    flat = (surf, cor)
    tiles_n = [ref[N - 8 : N, :] for ref in flat] + [deep[PAD + N - 8 : PAD + N, :]]
    tiles_s = [ref[0:8, :] for ref in flat] + [deep[PAD : PAD + 8, :]]
    for i in range(3):
        send1[0, i] = to_e[i]
        send1[1, i] = to_w[i]
        send1[2, i] = tiles_n[i]
        send1[3, i] = tiles_s[i]
    for t in range(3):
        a, b = edge[2 * t], edge[2 * t + 1]
        send1[0, 3 + t] = jnp.where(even, a, pltpu.roll(b, 1, 1))
        send1[1, 3 + t] = jnp.where(even, pltpu.roll(b, N - 1, 1), a)
        send1[2, 3 + t] = row_n[t]
        send1[3, 3 + t] = row_s[t]
    for i, tile in enumerate((rows_e, rows_w, cols_n, cols_s)):
        send1[i, 6] = tile
    corner_n, corner_s = pack_ends(tiles_n), pack_ends(tiles_s)
    for i, tiles in enumerate((
        (rows_e, cols_n, corner_n[0]), (rows_w, cols_n, corner_n[1]),
        (rows_e, cols_s, corner_s[0]), (rows_w, cols_s, corner_s[1]),
    )):
        for j, tile in enumerate(tiles):
            send_d1[i, j] = tile
    swap[16] = by_index(row)

    copies = {}

    def send(name, source, target, slot, other):
        copy = pltpu.make_async_remote_copy(
            src_ref=source, dst_ref=target, send_sem=send_sem.at[slot], recv_sem=recv_sem.at[slot],
            device_id=other, device_id_type=MESH,
        )
        copy.start()
        copies[name] = copy

    pl.semaphore_wait(barrier, 9)
    for i in range(4):
        send(("d1", i), send_d1.at[i], recv_d1.at[3 - i], 3 + i, diagonal[i])
    for i in range(4):
        send(("s1", i), send1.at[i], recv1.at[TURNED[i]], 7 + i, straight[i])

    def chunk(i, carry):
        rows = 16
        at = pl.multiple_of(i * rows, rows)
        lane16 = lanes(rows)
        d = deep[pl.ds(at + PAD, rows), :]
        d_e = jnp.where(lane16 == N - 1, 0.0, jnp.minimum(d, pltpu.roll(d, N - 1, 1)))
        d_n = jnp.minimum(d, deep[pl.ds(at + PAD + 1, rows), :])
        d_s = jnp.minimum(d, deep[pl.ds(at + PAD - 1, rows), :])
        f = cor[pl.ds(at, rows), :]
        sums = [jnp.zeros((rows, N), jnp.float32) for _ in range(4)]
        for k in range(LEVELS):
            level = first_level + k
            here, on_e, on_n, on_s = (level < other for other in (d, d_e, d_n, d_s))
            start = k * PITCH + PAD + at

            def around(ref):
                c = ref[pl.ds(start, rows), :]
                e = jnp.where(on_e, pltpu.roll(c, N - 1, 1) - c, 0.0)
                n = jnp.where(on_n, ref[pl.ds(start + 1, rows), :] - c, 0.0)
                s = jnp.where(on_s, c - ref[pl.ds(start - 1, rows), :], 0.0)
                return c, e, pltpu.roll(e, 1, 1), n, s

            ve, e_e, e_w, e_n, e_s = around(levels_e)
            vn, n_e, n_w, n_n, n_s = around(levels_n)
            _, p_e, p_w, p_n, p_s = around(levels_p)
            masked_e = jnp.where(here, ve, 0.0)
            masked_n = jnp.where(here, vn, 0.0)
            tend_e = f * masked_n + VISCOSITY * ((e_e - e_w) + (e_n - e_s)) - 0.5 * (p_e + p_w)
            tend_n = VISCOSITY * ((n_e - n_w) + (n_n - n_s)) - 0.5 * (p_n + p_s) - f * masked_e
            base_e[pl.ds(k * N + at, rows), :] = masked_e + tend_e
            base_n[pl.ds(k * N + at, rows), :] = masked_n + tend_n
            weight = thick[k]
            for slot, value in enumerate((masked_e, masked_n, tend_e, tend_n)):
                sums[slot] += weight * value
        for slot in range(4):
            part[slot, pl.ds(at, rows), :] = sums[slot]
        return carry

    lax.fori_loop(0, N // 16, chunk, 0)
    to_e, to_w = strips([(part.at[slot], 0) for slot in range(4)])
    for f in range(4):
        swap[f] = to_e[f]
        swap[4 + f] = to_w[f]
        swap[8 + f] = part[f, N - 8 : N, :]
        swap[12 + f] = part[f, 0:8, :]
    send("swap", swap, swap_in, 0, sister)
    send("part", part, part_in, 1, sister)

    copies["swap"].wait_recv()
    whole = [swap[j] + swap_in[j] for j in range(16)]
    for i in range(4):
        for f in range(4):
            send2[i, f] = whole[4 * i + f]
    ends_n, ends_s = pack_ends(whole[8:12]), pack_ends(whole[12:16])
    for i, tile in enumerate((*ends_n, *ends_s)):
        send_d2[i] = tile
    for i in range(4):
        send(("d2", i), send_d2.at[i], recv_d2.at[3 - i], 11 + i, diagonal[i])
    for i in range(4):
        send(("s2", i), send2.at[i], recv2.at[TURNED[i]], 15 + i, straight[i])

    upper = gz == 1
    own_thick, other_thick = 0.5 * COURANT * swap[16], 0.5 * COURANT * swap_in[16]
    thick_low = jnp.where(upper, other_thick, own_thick)
    thick_high = jnp.where(upper, own_thick, other_thick)

    def depth_of(d):
        out = jnp.zeros_like(d)
        for k in range(2 * LEVELS):
            tile = thick_low if k < LEVELS else thick_high
            weight = jnp.broadcast_to(tile[k % LEVELS : k % LEVELS + 1, :], d.shape)
            out = out + jnp.where(k < d, weight, 0.0)
        return out

    def settle(ref, at, rows):
        d = ref[DEEPEST, pl.ds(at, rows), :]
        ref[DEPTH, pl.ds(at, rows), :] = depth_of(d)
        ref[OCEAN, pl.ds(at, rows), :] = jnp.where(d > 0.0, 1.0, 0.0)

    xm[HEIGHT, TOP : TOP + N, :] = surf[...]
    xm[CORIOLIS, TOP : TOP + N, :] = COURANT * cor[...]
    xm[DEEPEST, TOP : TOP + N, :] = deep[PAD : PAD + N, :]

    def settle_main(i, carry):
        settle(xm, pl.multiple_of(TOP + 32 * i, 8), 32)
        return carry

    lax.fori_loop(0, N // 32, settle_main, 0)
    copies["part"].wait_recv()
    for f in range(4):
        whole_f = part[f] + part_in[f]
        xm[EAST + f, TOP : TOP + N, :] = whole_f if f < 2 else COURANT * whole_f
        if f < 2:
            totals[f] = whole_f

    for i in range(4):
        copies["d1", i].wait_recv()
        copies["s1", i].wait_recv()
    from_e, from_w, from_n, from_s = (recv1.at[i] for i in range(4))

    def beside(tile_e, tile_w, index):
        turn = (N - 8 * (index + 1)) % N if isinstance(index, int) else lax.rem(2 * N - 8 * (index + 1), N)
        return jnp.where(left_half, pltpu.roll(tile_e, turn, 1), pltpu.roll(tile_w, turn, 1))

    def put(ref, f, at, tile):
        ref[f, at, :] = COURANT * tile if f in (CORIOLIS, F_EAST, F_NORTH) else tile

    beyond_n, beyond_s = pl.ds(TOP + N, 8), pl.ds(TOP - 8, 8)
    d_north = beside(recv_d1[0, 2], recv_d1[1, 2], 2)
    d_south = beside(recv_d1[2, 2], recv_d1[3, 2], 2)
    d_first, d_last = (beside(from_e[2], from_w[2], g) for g in (0, 15))

    east_of = lane & 1
    sign = jnp.where(even, -0.5, 0.5)
    in_group = lane & 7

    strip_d = jnp.where(
        in_group == 0, pltpu.roll(from_e[2], N - 8, 1),
        jnp.where(in_group == 1, pltpu.roll(from_w[2], N - 6, 1), 0.0),
    )
    strip_d = strip_d + pltpu.roll(strip_d, 2, 1)
    strip_d = strip_d + pltpu.roll(strip_d, 4, 1)
    own_d = edges[6]
    column_terms = []
    sums_g = sums_e = sums_n = zero
    for half in range(2):
        level_in = (in_group >> 1) + 4 * half
        level = level_in.astype(jnp.float32) + first_level
        both = (level < own_d) & (level < strip_d)
        weight = by_index(level_in)
        diff = []
        for t in range(3):
            if half == 0:
                halo = jnp.where(even, pltpu.roll(from_e[3 + t], N - 1, 1), pltpu.roll(from_w[3 + t], 1, 1))
            else:
                halo = jnp.where(even, from_e[3 + t], from_w[3 + t])
            diff.append(jnp.where(both, halo - edges[2 * t + half], 0.0))
        drag_e, drag_n, grad = VISCOSITY * diff[0], VISCOSITY * diff[1], sign * diff[2]
        column_terms.append((grad + drag_e, drag_n))
        sums_g = sums_g + weight * grad
        sums_e = sums_e + weight * drag_e
        sums_n = sums_n + weight * drag_n

    def over_levels(v):
        v = v + pltpu.roll(v, N - 2, 1)
        return v + pltpu.roll(v, N - 4, 1)

    def swapped(v):
        return jnp.where(even, pltpu.roll(v, N - 1, 1), pltpu.roll(v, 1, 1))

    sums_g, sums_e, sums_n = over_levels(sums_g), over_levels(sums_e), over_levels(sums_n)
    late[0] = jnp.where(
        in_group < 2, sums_g + sums_e,
        jnp.where(
            in_group < 4, pltpu.roll(sums_n, 2, 1),
            jnp.where(
                in_group < 6, pltpu.roll(swapped(sums_g - sums_e), 4, 1), pltpu.roll(swapped(-sums_n), 6, 1)
            ),
        ),
    )

    in_tile = (lane & 15) >> 1
    tile_level = in_tile.astype(jnp.float32) + first_level
    tile_weight = by_index(in_tile) * jnp.where(lane < 32, VISCOSITY, sign)
    for slot, (tile, ahead, behind, side, near, far) in enumerate((
        (from_n[6], recv_d1[0, 1], recv_d1[1, 1], d_north, from_n[2], N - 8),
        (from_s[6], recv_d1[2, 1], recv_d1[3, 1], d_south, from_s[2], 0),
    )):

        def ends(v, a, b):
            return jnp.where(
                even, jnp.broadcast_to(v[:, a : a + 1], (8, N)), jnp.broadcast_to(v[:, b : b + 1], (8, N))
            )

        both = (tile_level < ends(near, N - 1, 0)) & (tile_level < ends(side, 0, N - 1))
        halo = jnp.where(even, pltpu.roll(ahead, N - 1, 1), pltpu.roll(behind, 1, 1))
        diff = halo - tile
        if far:
            diff = pltpu.roll(diff, far, 1)
        v = over_levels(jnp.where(both, tile_weight * diff, 0.0))
        late[1 + slot] = v + pltpu.roll(v, N - 8, 1)

    row_level = row.astype(jnp.float32) + first_level
    row_weight = by_index(row)

    def row_pairs(own, halo, d_own, d_halo, factor):
        both = (row_level < d_own) & (row_level < d_halo)
        diff = [jnp.where(both, h - o, 0.0) for h, o in zip(halo, own)]
        return factor * diff[2], VISCOSITY * diff[0], VISCOSITY * diff[1]

    def spread_row(v):
        return jnp.broadcast_to(v, (8, N))

    own_rows_n = [ref[pl.ds(PAD + N - 1, LEVELS, stride=PITCH), :] for ref in levels]
    own_rows_s = [ref[pl.ds(PAD, LEVELS, stride=PITCH), :] for ref in levels]
    main_n = row_pairs(
        own_rows_n, [from_n[3 + t] for t in range(3)],
        spread_row(deep[PAD + N - 1 : PAD + N, :]), spread_row(from_n[2, 0:1, :]), -0.5,
    )
    main_s = row_pairs(
        own_rows_s, [from_s[3 + t] for t in range(3)],
        spread_row(deep[PAD : PAD + 1, :]), spread_row(from_s[2, 7:8, :]), 0.5,
    )
    side_n = row_pairs(
        [beside(from_e[6], from_w[6], 2 * t) for t in range(3)],
        [beside(recv_d1[0, 0], recv_d1[1, 0], 2 * t + 1) for t in range(3)],
        spread_row(d_last[7:8, :]), spread_row(d_north[0:1, :]), -0.5,
    )
    side_s = row_pairs(
        [beside(from_e[6], from_w[6], 2 * t + 1) for t in range(3)],
        [beside(recv_d1[2, 0], recv_d1[3, 0], 2 * t) for t in range(3)],
        spread_row(d_first[0:1, :]), spread_row(d_south[7:8, :]), 0.5,
    )
    for slot, pairs in ((3, (main_n, main_s)), (4, (side_n, side_s))):
        tile = zero
        for i, terms in enumerate(pairs):
            for j, term in enumerate(terms):
                total = jnp.sum(row_weight * term, axis=0, keepdims=True)
                tile = jnp.where(row == 3 * i + j, spread_row(total), tile)
        late[slot] = tile
    send("late", late, late_in, 2, sister)

    for at, (grad, drag_e, drag_n) in ((N - 1, main_n), (0, main_s)):
        where_ = pl.ds(at, LEVELS, stride=N)
        base_e[where_, :] = base_e[where_, :] + drag_e
        base_n[where_, :] = base_n[where_, :] + (grad + drag_n)
    for half in range(2):
        for j in range(2):
            edges[2 * half + j] = column_terms[half][j]
    outer = (lane == 0) | (lane == N - 1)

    def add_columns(g, carry):
        for k in range(LEVELS):
            at = pl.multiple_of(g * 8 + k * N, 8)
            turn = (N - 1 - 2 * (k % 4)) - 8 * g
            for j, ref in enumerate((base_e, base_n)):
                v = pltpu.roll(edges[2 * (k // 4) + j], turn, 1)
                ref[pl.ds(at, 8), :] = ref[pl.ds(at, 8), :] + jnp.where(outer, v, 0.0)
        return carry

    for f in range(3):
        put(xm, f, beyond_n, from_n[f])
        put(xm, f, beyond_s, from_s[f])
        put(xs, f, beyond_n, beside(recv_d1[0, 2], recv_d1[1, 2], f))
        put(xs, f, beyond_s, beside(recv_d1[2, 2], recv_d1[3, 2], f))

    def unpack_inputs(g, carry):
        at = pl.multiple_of(TOP + 8 * g, 8)
        for f in range(3):
            put(xs, f, pl.ds(at, 8), beside(from_e[f], from_w[f], g))
        return carry

    each_group(unpack_inputs)
    each_group(add_columns)

    def settle_side(i, carry):
        settle(xs, pl.multiple_of(8 + 48 * i, 8), 48)
        return carry

    lax.fori_loop(0, 3, settle_side, 0)
    settle(xm, TOP - 8, 8)
    settle(xm, TOP + N, 8)

    def add_to(ref, field, at, value):
        ref[field, at, :] = ref[field, at, :] + value

    copies["late"].wait_recv()
    column_sum = COURANT * (late[0] + late_in[0])

    def place_columns(g, carry):
        at = pl.ds(pl.multiple_of(TOP + 8 * g, 8), 8)
        for f in range(2):
            turn = (N - 1 - 2 * f) - 8 * g
            add_to(xm, F_EAST + f, at, jnp.where(outer, pltpu.roll(column_sum, turn, 1), 0.0))
            xs[F_EAST + f, at, :] = jnp.where(outer, pltpu.roll(column_sum, turn - 4, 1), 0.0)
        return carry

    each_group(place_columns)
    for slot, at in ((1, beyond_n), (2, beyond_s)):
        v = COURANT * (late[slot] + late_in[slot])
        drag_e, drag_n, grad = v, pltpu.roll(v, N - 16, 1), pltpu.roll(v, N - 32, 1)
        xm[F_EAST, at, :] = jnp.where(outer, pltpu.roll(grad + drag_e, N - 1, 1), 0.0)
        xm[F_NORTH, at, :] = jnp.where(outer, pltpu.roll(drag_n, N - 1, 1), 0.0)
        xs[F_EAST, at, :] = jnp.where(outer, pltpu.roll(swapped(grad - drag_e), N - 1, 1), 0.0)
        xs[F_NORTH, at, :] = jnp.where(outer, pltpu.roll(swapped(-drag_n), N - 1, 1), 0.0)
    for slot, ref in ((3, xm), (4, xs)):
        v = COURANT * (late[slot] + late_in[slot])
        for i, (own, halo) in enumerate(((TOP + N - 1, TOP + N), (TOP, TOP - 1))):
            grad, drag_e, drag_n = (v[3 * i + j : 3 * i + j + 1, :] for j in range(3))
            add_to(ref, F_EAST, pl.ds(own, 1), drag_e)
            add_to(ref, F_NORTH, pl.ds(own, 1), grad + drag_n)
            add_to(ref, F_EAST, pl.ds(halo, 1), -drag_e)
            add_to(ref, F_NORTH, pl.ds(halo, 1), grad - drag_n)

    for i in range(4):
        copies["d2", i].wait_recv()
        copies["s2", i].wait_recv()

    def put_sum(ref, f, at, tile):
        if f < 2:
            ref[EAST + f, at, :] = tile
        else:
            add_to(ref, EAST + f, at, COURANT * tile)

    for f in range(4):
        put_sum(xm, f, beyond_n, recv2[2, f])
        put_sum(xm, f, beyond_s, recv2[3, f])
        put_sum(xs, f, beyond_n, beside(recv_d2[0], recv_d2[1], f))
        put_sum(xs, f, beyond_s, beside(recv_d2[2], recv_d2[3], f))

    def unpack_sums(g, carry):
        at = pl.ds(pl.multiple_of(TOP + 8 * g, 8), 8)
        for f in range(4):
            put_sum(xs, f, at, beside(recv2[0, f], recv2[1, f], g))
        return carry

    each_group(unpack_sums)

    rows = 48
    lane_r = lanes(rows)
    for step in range(SUBSTEPS):
        for at in range(8, 8 + 3 * rows, rows):
            here = slice(at, at + rows)
            up, down = slice(at + 1, at + rows + 1), slice(at - 1, at + rows - 1)
            main, side = xm[EAST, here, :], xs[EAST, here, :]
            e = shift_east(main, side, lane_r)
            w = shift_west(main, side, lane_r)
            for ref, e_, w_ in ((xm, e[0], w[0]), (xs, e[1], w[1])):
                spread = (e_ - w_) + (ref[NORTH, up, :] - ref[NORTH, down, :])
                ref[HEIGHT, here, :] = ref[OCEAN, here, :] * (ref[HEIGHT, here, :] - (0.5 * COURANT) * spread)
        for at in range(8, 8 + 3 * rows, rows):
            here = slice(at, at + rows)
            up, down = slice(at + 1, at + rows + 1), slice(at - 1, at + rows - 1)
            main, side = xm[HEIGHT, here, :], xs[HEIGHT, here, :]
            e = shift_east(main, side, lane_r)
            w = shift_west(main, side, lane_r)
            for ref, e_, w_ in ((xm, e[0], w[0]), (xs, e[1], w[1])):
                if ref is xs and step == SUBSTEPS - 1:
                    continue
                old_e, old_n = ref[EAST, here, :], ref[NORTH, here, :]
                depth, f = ref[DEPTH, here, :], ref[CORIOLIS, here, :]
                ref[EAST, here, :] = (old_e + ref[F_EAST, here, :]) + (f * old_n - depth * (e_ - w_))
                ref[NORTH, here, :] = (old_n + ref[F_NORTH, here, :]) - (
                    f * old_e + depth * (ref[HEIGHT, up, :] - ref[HEIGHT, down, :])
                )

    block = slice(TOP, TOP + N)
    floor_depth = (2.0 / COURANT) * xm[DEPTH, block, :] + (1.0 - xm[OCEAN, block, :])
    for f in range(2):
        forced = (TIMESTEP / COURANT) * xm[F_EAST + f, block, :]
        corr[f] = (xm[EAST + f, block, :] - totals[f] - forced) / floor_depth
    height_out[...] = xm[HEIGHT, block, :]
    for copy in copies.values():
        copy.wait_send()


def finish(base_e, base_n, corr, height, deep, height_h, east_h, north_h, outs, sem):
    copies = [pltpu.make_async_copy(height, height_h, sem.at[2 * LEVELS])]
    copies[0].start()
    first_level = (lax.axis_index("gz") * LEVELS).astype(jnp.float32)
    for k in range(LEVELS):
        at = pl.ds(k * N, N)
        wet = first_level + k < deep[...]
        for f, (base, target) in enumerate(((base_e, east_h), (base_n, north_h))):
            outs[f, at, :] = jnp.where(wet, base[at, :] + corr[f], 0.0)
            copy = pltpu.make_async_copy(outs.at[f, at], target.at[at], sem.at[2 * k + f])
            copy.start()
            copies.append(copy)
    for copy in copies:
        copy.wait()


def on_device(
    layer_east, layer_north, layer_press, surface, land_sea, bottom_level, coriolis, level_thick
):
    f32 = jnp.float32
    tall = (LEVELS * N, N)
    flat = (N, N)
    hbm, vmem = pl.BlockSpec(memory_space=pltpu.HBM), pl.BlockSpec(memory_space=pltpu.VMEM)
    between = pl.pallas_call(
        kernel,
        name="ocean",
        out_shape=tuple(jax.ShapeDtypeStruct(shape, f32) for shape in (tall, tall, (2, *flat), flat, flat)),
        in_specs=[hbm] * 8,
        out_specs=(vmem,) * 5,
        scratch_shapes=[
            pltpu.SMEM((LEVELS,), f32),
            *[pltpu.VMEM((LEVELS * PITCH, N), f32)] * 3,
            pltpu.VMEM((PITCH, N), f32),
            *[pltpu.VMEM(flat, f32)] * 2,
            *[pltpu.VMEM(flat, jnp.int32)] * 2,
            pltpu.VMEM((7, 8, N), f32),
            *[pltpu.VMEM((4, N, N), f32)] * 2,
            *[pltpu.VMEM((17, 8, N), f32)] * 2,
            *[pltpu.VMEM((5, 8, N), f32)] * 2,
            pltpu.VMEM((2, N, N), f32),
            *[
                pltpu.VMEM(shape, f32)
                for _ in range(2)
                for shape in ((4, 7, 8, N), (4, 4, 8, N), (4, 3, 8, N), (4, 8, N))
            ],
            *[pltpu.VMEM((9, EXT, N), f32)] * 2,
            pltpu.SemaphoreType.DMA((29,)),
            pltpu.SemaphoreType.DMA((19,)),
            pltpu.SemaphoreType.DMA((19,)),
        ],
        compiler_params=pltpu.CompilerParams(
            collective_id=0, has_side_effects=True, vmem_limit_bytes=VMEM_LIMIT
        ),
    )(
        *(
            pltpu.with_memory_space_constraint(x, pltpu.HBM)
            for x in (
                level_thick,
                layer_east.reshape(tall),
                layer_north.reshape(tall),
                layer_press.reshape(tall),
                surface,
                land_sea,
                bottom_level,
                coriolis,
            )
        )
    )
    height, east_next, north_next = pl.pallas_call(
        finish,
        name="finish",
        out_shape=tuple(jax.ShapeDtypeStruct(shape, f32) for shape in (flat, tall, tall)),
        in_specs=[vmem] * 5,
        out_specs=(hbm,) * 3,
        scratch_shapes=[pltpu.VMEM((2, *tall), f32), pltpu.SemaphoreType.DMA((2 * LEVELS + 1,))],
        compiler_params=pltpu.CompilerParams(vmem_limit_bytes=VMEM_LIMIT),
    )(*between)
    shape = (LEVELS, N, N)
    return height, east_next.reshape(shape), north_next.reshape(shape)


def solution(mesh):
    whole, flat = P("gz", "gy", "gx"), P("gy", "gx")
    return jax.shard_map(
        on_device,
        mesh=mesh,
        in_specs=(whole, whole, whole, flat, flat, flat, flat, P("gz")),
        out_specs=(flat, whole, whole),
        check_vma=False,
    )
```

```python
import jax
import jax.numpy as jnp
from jax import lax
from jax.experimental import pallas as pl
from jax.experimental.pallas import tpu as pltpu
from jax.sharding import PartitionSpec as P

MESH = pl.DeviceIdType.MESH
SUBSTEPS = 4
COURANT = 0.25
VISCOSITY = 0.1
TIMESTEP = SUBSTEPS * COURANT
assert TIMESTEP == 1.0
VMEM_LIMIT = 16 * 2**20

N = 128
LEVELS = 8
PITCH = 144
PAD = 8
TOP = 16
EXT = 160

HEIGHT, CORIOLIS, DEEPEST, EAST, NORTH, F_EAST, F_NORTH, DEPTH, OCEAN = range(9)
TURNED = (1, 0, 3, 2)


def shift_east(main, side, lane):
    a, b = pltpu.roll(main, N - 1, 1), pltpu.roll(side, N - 1, 1)
    last = lane == N - 1
    return jnp.where(last, b, a), jnp.where(last, a, b)


def shift_west(main, side, lane):
    a, b = pltpu.roll(main, 1, 1), pltpu.roll(side, 1, 1)
    first = lane == 0
    return jnp.where(first, b, a), jnp.where(first, a, b)


def lanes(rows):
    return lax.broadcasted_iota(jnp.int32, (rows, N), 1)


def kernel(
    thick_h, east_h, north_h, press_h, surf_h, land_h, bottom_h, cor_h,
    base_e, base_n, corr, height_out, deep_out,
    thick, levels_e, levels_n, levels_p, deep, surf, cor, land, bottom,
    edges, part, part_in, swap, swap_in, late, late_in, totals,
    send1, send2, send_d1, send_d2, recv1, recv2, recv_d1, recv_d2,
    xm, xs, load_sem, send_sem, recv_sem,
):
    gx, gy, gz = lax.axis_index("gx"), lax.axis_index("gy"), lax.axis_index("gz")
    nx, ny = lax.axis_size("gx"), lax.axis_size("gy")
    east, west = lax.rem(gx + 1, nx), lax.rem(gx + nx - 1, nx)
    north, south = lax.rem(gy + 1, ny), lax.rem(gy + ny - 1, ny)
    sister = {"gz": 1 - gz}
    straight = ({"gx": east}, {"gx": west}, {"gy": north}, {"gy": south})
    diagonal = (
        {"gx": east, "gy": north}, {"gx": west, "gy": north},
        {"gx": east, "gy": south}, {"gx": west, "gy": south},
    )

    barrier = pltpu.get_barrier_semaphore()
    for other in (*diagonal, *straight, sister):
        pl.semaphore_signal(barrier, inc=1, device_id=other, device_id_type=MESH)

    loads = []

    def load(source, target):
        copy = pltpu.make_async_copy(source, target, load_sem.at[len(loads)])
        copy.start()
        loads.append(copy)

    load(thick_h, thick)
    load(land_h, land)
    load(bottom_h, bottom)
    load(surf_h, surf)
    load(cor_h, cor)
    levels = (levels_e, levels_n, levels_p)
    for source, target in zip((east_h, north_h, press_h), levels):
        for k in range(LEVELS):
            load(source.at[pl.ds(k * N, N)], target.at[pl.ds(k * PITCH + PAD, N)])

    lane = lanes(8)
    even = (lane & 1) == 0
    row = lax.broadcasted_iota(jnp.int32, (8, N), 0)
    first_level = (gz * LEVELS).astype(jnp.float32)
    zero = jnp.zeros((8, N), jnp.float32)

    def by_index(index):
        out = zero
        for k in range(LEVELS):
            out = jnp.where(index == k, thick[k], out)
        return out

    for copy in loads[:5]:
        copy.wait()
    deep[0:PAD, :] = zero
    deep[PAD + N : PITCH, :] = zero
    deepest = land[...].astype(jnp.float32) * bottom[...].astype(jnp.float32)
    deep[PAD : PAD + N, :] = deepest
    deep_out[...] = deepest

    def each_group(body, carry=()):
        def trip(i, carry):
            for u in range(4):
                carry = body(4 * i + u, carry)
            return carry

        return lax.fori_loop(0, 4, trip, carry)

    def strips(refs):
        def body(g, carry):
            to_east = (lane >> 3) == g
            to_west = (lane >> 3) == lax.rem(g + 1, 16)
            turn = lax.rem(8 * g + 8, N)
            out = []
            for i, (ref, pad) in enumerate(refs):
                v = pltpu.roll(ref[pl.ds(pl.multiple_of(g * 8 + pad, 8), 8), :], turn, 1)
                out += [jnp.where(to_east, v, carry[2 * i]), jnp.where(to_west, v, carry[2 * i + 1])]
            return tuple(out)

        tiles = each_group(body, (zero,) * (2 * len(refs)))
        return tiles[0::2], tiles[1::2]

    flat_e, flat_w = strips([(surf, 0), (cor, 0), (deep, PAD)])

    def pack_deepest(g, d_edge):
        v = pltpu.roll(deep[pl.ds(pl.multiple_of(g * 8 + PAD, 8), 8), :], 8 * g + 1, 1)
        return jnp.where(((lane - 8 * g) >> 1) == 0, v, d_edge)

    d_edge = each_group(pack_deepest, zero)
    d_edge = d_edge + pltpu.roll(d_edge, 2, 1)
    d_edge = d_edge + pltpu.roll(d_edge, 4, 1)
    edges[6] = d_edge

    edge = []
    for t, ref in enumerate(levels):
        for copy in loads[5 + LEVELS * t : 5 + LEVELS * (t + 1)]:
            copy.wait()

        def pack(g, carry, ref=ref):
            carry = list(carry)
            pair = (lane - 8 * g) >> 1
            for k in range(LEVELS):
                at = pl.multiple_of(g * 8 + (k * PITCH + PAD), 8)
                v = pltpu.roll(ref[pl.ds(at, 8), :], 8 * g + 2 * (k % 4) + 1, 1)
                carry[k // 4] = jnp.where(pair == k % 4, v, carry[k // 4])
            return tuple(carry)

        edge += each_group(pack, (zero, zero))
    for j in range(6):
        edges[j] = edge[j]
    row_n = [ref[pl.ds(PAD + N - 1, LEVELS, stride=PITCH), :] for ref in levels]
    row_s = [ref[pl.ds(PAD, LEVELS, stride=PITCH), :] for ref in levels]

    def pack_ends(tiles):
        high = low = zero
        for j, v in enumerate(tiles):
            v = pltpu.roll(v, 8 * j + 8, 1)
            high = jnp.where((lane >> 3) == j, v, high)
            low = jnp.where((lane >> 3) == j + 1, v, low)
        return high, low

    rows_e, rows_w = pack_ends([r for t in range(3) for r in (row_n[t], row_s[t])])
    cols_n, cols_s = pack_ends(edge)
    flat = (surf, cor)
    tiles_n = [ref[N - 8 : N, :] for ref in flat] + [deep[PAD + N - 8 : PAD + N, :]]
    tiles_s = [ref[0:8, :] for ref in flat] + [deep[PAD : PAD + 8, :]]
    for i, tile in enumerate((flat_e[2], flat_w[2], tiles_n[2], tiles_s[2])):
        send1[i, 0] = tile
    for t in range(3):
        a, b = edge[2 * t], edge[2 * t + 1]
        send1[0, 1 + t] = jnp.where(even, a, pltpu.roll(b, 1, 1))
        send1[1, 1 + t] = jnp.where(even, pltpu.roll(b, N - 1, 1), a)
        send1[2, 1 + t] = row_n[t]
        send1[3, 1 + t] = row_s[t]
    for i, tile in enumerate((rows_e, rows_w, cols_n, cols_s)):
        send1[i, 4] = tile
    for i, tiles in enumerate((flat_e, flat_w, tiles_n, tiles_s)):
        for f in range(2):
            send2[i, 4 + f] = tiles[f]
    ends_n = pack_ends([v for pair in zip(row_n, tiles_n) for v in pair])
    ends_s = pack_ends([v for pair in zip(row_s, tiles_s) for v in pair])
    for i, (ends, columns) in enumerate((
        (ends_n[0], cols_n), (ends_n[1], cols_n), (ends_s[0], cols_s), (ends_s[1], cols_s)
    )):
        send_d1[i] = jnp.where(lane < 64, ends, pltpu.roll(columns, 64, 1))

    swap[16] = by_index(row)

    copies = {}

    def send(name, source, target, slot, other):
        copy = pltpu.make_async_remote_copy(
            src_ref=source, dst_ref=target, send_sem=send_sem.at[slot], recv_sem=recv_sem.at[slot],
            device_id=other, device_id_type=MESH,
        )
        copy.start()
        copies[name] = copy

    pl.semaphore_wait(barrier, 9)
    for i in range(4):
        send(("d1", i), send_d1.at[i], recv_d1.at[3 - i], 3 + i, diagonal[i])
    for i in range(4):
        send(("s1", i), send1.at[i], recv1.at[TURNED[i]], 7 + i, straight[i])


    def chunk(i, carry):
        rows = 8
        at = pl.multiple_of(i * rows, rows)
        lane16 = lanes(rows)
        d = deep[pl.ds(at + PAD, rows), :]
        d_e = jnp.where(lane16 == N - 1, 0.0, jnp.minimum(d, pltpu.roll(d, N - 1, 1)))
        d_w = jnp.where(lane16 == 0, 0.0, jnp.minimum(d, pltpu.roll(d, 1, 1)))
        d_n = jnp.minimum(d, deep[pl.ds(at + PAD + 1, rows), :])
        d_s = jnp.minimum(d, deep[pl.ds(at + PAD - 1, rows), :])
        f = cor[pl.ds(at, rows), :]
        sums = [jnp.zeros((rows, N), jnp.float32) for _ in range(4)]
        for k in range(LEVELS):
            level = first_level + k
            here, on_e, on_w, on_n, on_s = (level < other for other in (d, d_e, d_w, d_n, d_s))
            start = k * PITCH + PAD + at

            ve, vn, p = (ref[pl.ds(start, rows), :] for ref in levels)

            def along_y(ref, c):
                n = jnp.where(on_n, ref[pl.ds(start + 1, rows), :] - c, 0.0)
                return n, jnp.where(on_s, c - ref[pl.ds(start - 1, rows), :], 0.0)

            drag, half_p = VISCOSITY * ve, 0.5 * p
            ahead, behind = drag - half_p, drag + half_p
            x_e = jnp.where(on_e, pltpu.roll(ahead, N - 1, 1) - ahead, 0.0)
            x_w = jnp.where(on_w, behind - pltpu.roll(behind, 1, 1), 0.0)
            n_e = jnp.where(on_e, pltpu.roll(vn, N - 1, 1) - vn, 0.0)
            n_w = pltpu.roll(n_e, 1, 1)
            e_n, e_s = along_y(levels_e, ve)
            n_n, n_s = along_y(levels_n, vn)
            p_n, p_s = along_y(levels_p, p)
            masked_e = jnp.where(here, ve, 0.0)
            masked_n = jnp.where(here, vn, 0.0)
            tend_e = (x_e - x_w) + VISCOSITY * (e_n - e_s) + f * masked_n
            tend_n = VISCOSITY * ((n_e - n_w) + (n_n - n_s)) - 0.5 * (p_n + p_s) - f * masked_e
            base_e[pl.ds(k * N + at, rows), :] = masked_e + tend_e
            base_n[pl.ds(k * N + at, rows), :] = masked_n + tend_n
            weight = thick[k]
            for slot, value in enumerate((masked_e, masked_n, tend_e, tend_n)):
                sums[slot] += weight * value
        for slot in range(4):
            part[slot, pl.ds(at, rows), :] = sums[slot]
        return carry

    lax.fori_loop(0, N // 8, chunk, 0)
    to_e, to_w = strips([(part.at[slot], 0) for slot in range(4)])
    for f in range(4):
        swap[f] = to_e[f]
        swap[4 + f] = to_w[f]
        swap[8 + f] = part[f, N - 8 : N, :]
        swap[12 + f] = part[f, 0:8, :]
    send("swap", swap, swap_in, 0, sister)

    copies["swap"].wait_recv()
    whole = [swap[j] + swap_in[j] for j in range(16)]
    for i in range(4):
        for f in range(4):
            send2[i, f] = whole[4 * i + f]
    ends_n, ends_s = pack_ends(whole[8:12]), pack_ends(whole[12:16])
    for i, tile in enumerate((*ends_n, *ends_s)):
        send_d2[i] = tile
    for i in range(4):
        send(("d2", i), send_d2.at[i], recv_d2.at[3 - i], 11 + i, diagonal[i])
    for i in range(4):
        send(("s2", i), send2.at[i], recv2.at[TURNED[i]], 15 + i, straight[i])
    send("part", part, part_in, 1, sister)

    upper = gz == 1
    own_thick, other_thick = 0.5 * COURANT * swap[16], 0.5 * COURANT * swap_in[16]
    thick_low = jnp.where(upper, other_thick, own_thick)
    thick_high = jnp.where(upper, own_thick, other_thick)

    def depth_of(d):
        out = jnp.zeros_like(d)
        for k in range(2 * LEVELS):
            tile = thick_low if k < LEVELS else thick_high
            weight = jnp.broadcast_to(tile[k % LEVELS : k % LEVELS + 1, :], d.shape)
            out = out + jnp.where(k < d, weight, 0.0)
        return out

    def settle(ref, at, rows):
        d = ref[DEEPEST, pl.ds(at, rows), :]
        ref[DEPTH, pl.ds(at, rows), :] = depth_of(d)
        ref[OCEAN, pl.ds(at, rows), :] = jnp.where(d > 0.0, 1.0, 0.0)

    xm[HEIGHT, TOP : TOP + N, :] = surf[...]
    xm[CORIOLIS, TOP : TOP + N, :] = COURANT * cor[...]
    xm[DEEPEST, TOP : TOP + N, :] = deep[PAD : PAD + N, :]

    def settle_main(i, carry):
        settle(xm, pl.multiple_of(TOP + 32 * i, 8), 32)
        return carry

    lax.fori_loop(0, N // 32, settle_main, 0)
    copies["part"].wait_recv()
    for f in range(4):
        whole_f = part[f] + part_in[f]
        xm[EAST + f, TOP : TOP + N, :] = whole_f if f < 2 else COURANT * whole_f
        if f < 2:
            totals[f] = whole_f

    for i in range(4):
        copies["d1", i].wait_recv()
        copies["s1", i].wait_recv()
    from_e, from_w, from_n, from_s = (recv1.at[i] for i in range(4))

    def beside(tile_e, tile_w, index):
        following = lax.rem(index + 1, 16)
        both = jnp.where((lane >> 3) == following, tile_e, tile_w)
        return pltpu.roll(both, lax.rem(N - 8 * following, N), 1)

    def put(ref, f, at, tile):
        ref[f, at, :] = COURANT * tile if f in (CORIOLIS, F_EAST, F_NORTH) else tile

    beyond_n, beyond_s = pl.ds(TOP + N, 8), pl.ds(TOP - 8, 8)
    corners = [recv_d1[i] for i in range(4)]
    d_north = beside(corners[0], corners[1], 5)
    d_south = beside(corners[2], corners[3], 5)
    d_first, d_last = (beside(from_e[0], from_w[0], g) for g in (0, 15))

    east_of = lane & 1
    sign = jnp.where(even, -0.5, 0.5)
    in_group = lane & 7

    strip_d = jnp.where(
        in_group == 0, pltpu.roll(from_e[0], N - 8, 1),
        jnp.where(in_group == 1, pltpu.roll(from_w[0], N - 6, 1), 0.0),
    )
    strip_d = strip_d + pltpu.roll(strip_d, 2, 1)
    strip_d = strip_d + pltpu.roll(strip_d, 4, 1)
    own_d = edges[6]
    column_terms = []
    sums_g = sums_e = sums_n = zero
    for half in range(2):
        level_in = (in_group >> 1) + 4 * half
        level = level_in.astype(jnp.float32) + first_level
        both = (level < own_d) & (level < strip_d)
        weight = by_index(level_in)
        diff = []
        for t in range(3):
            if half == 0:
                halo = jnp.where(even, pltpu.roll(from_e[1 + t], N - 1, 1), pltpu.roll(from_w[1 + t], 1, 1))
            else:
                halo = jnp.where(even, from_e[1 + t], from_w[1 + t])
            diff.append(jnp.where(both, halo - edges[2 * t + half], 0.0))
        drag_e, drag_n, grad = VISCOSITY * diff[0], VISCOSITY * diff[1], sign * diff[2]
        column_terms.append((grad + drag_e, drag_n))
        sums_g = sums_g + weight * grad
        sums_e = sums_e + weight * drag_e
        sums_n = sums_n + weight * drag_n

    def over_levels(v):
        v = v + pltpu.roll(v, N - 2, 1)
        return v + pltpu.roll(v, N - 4, 1)

    def swapped(v):
        return jnp.where(even, pltpu.roll(v, N - 1, 1), pltpu.roll(v, 1, 1))

    sums_g, sums_e, sums_n = over_levels(sums_g), over_levels(sums_e), over_levels(sums_n)
    late[0] = jnp.where(
        in_group < 2, sums_g + sums_e,
        jnp.where(
            in_group < 4, pltpu.roll(sums_n, 2, 1),
            jnp.where(
                in_group < 6, pltpu.roll(swapped(sums_g - sums_e), 4, 1), pltpu.roll(swapped(-sums_n), 6, 1)
            ),
        ),
    )

    in_tile = (lane & 15) >> 1
    tile_level = in_tile.astype(jnp.float32) + first_level
    tile_weight = by_index(in_tile) * jnp.where(lane < 32, VISCOSITY, sign)
    for slot, (tile, ahead, behind, side, near, far) in enumerate((
        (from_n[4], corners[0], corners[1], d_north, from_n[0], N - 8),
        (from_s[4], corners[2], corners[3], d_south, from_s[0], 0),
    )):

        def ends(v, a, b):
            return jnp.where(
                even, jnp.broadcast_to(v[:, a : a + 1], (8, N)), jnp.broadcast_to(v[:, b : b + 1], (8, N))
            )

        both = (tile_level < ends(near, N - 1, 0)) & (tile_level < ends(side, 0, N - 1))
        halo = jnp.where(even, pltpu.roll(ahead, 63, 1), pltpu.roll(behind, 65, 1))
        diff = halo - tile
        if far:
            diff = pltpu.roll(diff, far, 1)
        v = over_levels(jnp.where(both, tile_weight * diff, 0.0))
        late[1 + slot] = v + pltpu.roll(v, N - 8, 1)

    row_level = row.astype(jnp.float32) + first_level
    row_weight = by_index(row)

    def row_pairs(own, halo, d_own, d_halo, factor):
        both = (row_level < d_own) & (row_level < d_halo)
        diff = [jnp.where(both, h - o, 0.0) for h, o in zip(halo, own)]
        return factor * diff[2], VISCOSITY * diff[0], VISCOSITY * diff[1]

    def spread_row(v):
        return jnp.broadcast_to(v, (8, N))

    own_rows_n = [ref[pl.ds(PAD + N - 1, LEVELS, stride=PITCH), :] for ref in levels]
    own_rows_s = [ref[pl.ds(PAD, LEVELS, stride=PITCH), :] for ref in levels]
    main_n = row_pairs(
        own_rows_n, [from_n[1 + t] for t in range(3)],
        spread_row(deep[PAD + N - 1 : PAD + N, :]), spread_row(from_n[0, 0:1, :]), -0.5,
    )
    main_s = row_pairs(
        own_rows_s, [from_s[1 + t] for t in range(3)],
        spread_row(deep[PAD : PAD + 1, :]), spread_row(from_s[0, 7:8, :]), 0.5,
    )
    side_n = row_pairs(
        [beside(from_e[4], from_w[4], 2 * t) for t in range(3)],
        [beside(corners[0], corners[1], 2 * t) for t in range(3)],
        spread_row(d_last[7:8, :]), spread_row(d_north[0:1, :]), -0.5,
    )
    side_s = row_pairs(
        [beside(from_e[4], from_w[4], 2 * t + 1) for t in range(3)],
        [beside(corners[2], corners[3], 2 * t) for t in range(3)],
        spread_row(d_first[0:1, :]), spread_row(d_south[7:8, :]), 0.5,
    )
    for slot, pairs in ((3, (main_n, main_s)), (4, (side_n, side_s))):
        tile = zero
        for i, terms in enumerate(pairs):
            for j, term in enumerate(terms):
                total = jnp.sum(row_weight * term, axis=0, keepdims=True)
                tile = jnp.where(row == 3 * i + j, spread_row(total), tile)
        late[slot] = tile
    send("late", late, late_in, 2, sister)

    for at, (grad, drag_e, drag_n) in ((N - 1, main_n), (0, main_s)):
        where_ = pl.ds(at, LEVELS, stride=N)
        base_e[where_, :] = base_e[where_, :] + drag_e
        base_n[where_, :] = base_n[where_, :] + (grad + drag_n)
    for half in range(2):
        for j in range(2):
            edges[2 * half + j] = column_terms[half][j]
    outer = (lane == 0) | (lane == N - 1)

    def add_columns(g, carry):
        for k in range(LEVELS):
            at = pl.multiple_of(g * 8 + k * N, 8)
            turn = (N - 1 - 2 * (k % 4)) - 8 * g
            for j, ref in enumerate((base_e, base_n)):
                v = pltpu.roll(edges[2 * (k // 4) + j], turn, 1)
                ref[pl.ds(at, 8), :] = ref[pl.ds(at, 8), :] + jnp.where(outer, v, 0.0)
        return carry

    put(xm, DEEPEST, beyond_n, from_n[0])
    put(xm, DEEPEST, beyond_s, from_s[0])
    for f in range(3):
        put(xs, f, beyond_n, beside(corners[0], corners[1], 2 * f + 1))
        put(xs, f, beyond_s, beside(corners[2], corners[3], 2 * f + 1))

    def unpack_deepest(g, carry):
        put(xs, DEEPEST, pl.ds(pl.multiple_of(TOP + 8 * g, 8), 8), beside(from_e[0], from_w[0], g))
        return carry

    each_group(unpack_deepest)
    each_group(add_columns)

    def settle_side(i, carry):
        settle(xs, pl.multiple_of(8 + 48 * i, 8), 48)
        return carry

    lax.fori_loop(0, 3, settle_side, 0)
    settle(xm, TOP - 8, 8)
    settle(xm, TOP + N, 8)

    def add_to(ref, field, at, value):
        ref[field, at, :] = ref[field, at, :] + value

    copies["late"].wait_recv()
    column_sum = COURANT * (late[0] + late_in[0])

    def place_columns(g, carry):
        at = pl.ds(pl.multiple_of(TOP + 8 * g, 8), 8)
        for f in range(2):
            turn = (N - 1 - 2 * f) - 8 * g
            add_to(xm, F_EAST + f, at, jnp.where(outer, pltpu.roll(column_sum, turn, 1), 0.0))
            xs[F_EAST + f, at, :] = jnp.where(outer, pltpu.roll(column_sum, turn - 4, 1), 0.0)
        return carry

    each_group(place_columns)
    for slot, at in ((1, beyond_n), (2, beyond_s)):
        v = COURANT * (late[slot] + late_in[slot])
        drag_e, drag_n, grad = v, pltpu.roll(v, N - 16, 1), pltpu.roll(v, N - 32, 1)
        xm[F_EAST, at, :] = jnp.where(outer, pltpu.roll(grad + drag_e, N - 1, 1), 0.0)
        xm[F_NORTH, at, :] = jnp.where(outer, pltpu.roll(drag_n, N - 1, 1), 0.0)
        xs[F_EAST, at, :] = jnp.where(outer, pltpu.roll(swapped(grad - drag_e), N - 1, 1), 0.0)
        xs[F_NORTH, at, :] = jnp.where(outer, pltpu.roll(swapped(-drag_n), N - 1, 1), 0.0)
    for slot, ref in ((3, xm), (4, xs)):
        v = COURANT * (late[slot] + late_in[slot])
        for i, (own, halo) in enumerate(((TOP + N - 1, TOP + N), (TOP, TOP - 1))):
            grad, drag_e, drag_n = (v[3 * i + j : 3 * i + j + 1, :] for j in range(3))
            add_to(ref, F_EAST, pl.ds(own, 1), drag_e)
            add_to(ref, F_NORTH, pl.ds(own, 1), grad + drag_n)
            add_to(ref, F_EAST, pl.ds(halo, 1), -drag_e)
            add_to(ref, F_NORTH, pl.ds(halo, 1), grad - drag_n)

    for i in range(4):
        copies["d2", i].wait_recv()
        copies["s2", i].wait_recv()

    def put_sum(ref, f, at, tile):
        if f < 2:
            ref[EAST + f, at, :] = tile
        else:
            add_to(ref, EAST + f, at, COURANT * tile)

    for f in range(4):
        put_sum(xm, f, beyond_n, recv2[2, f])
        put_sum(xm, f, beyond_s, recv2[3, f])
        put_sum(xs, f, beyond_n, beside(recv_d2[0], recv_d2[1], f))
        put_sum(xs, f, beyond_s, beside(recv_d2[2], recv_d2[3], f))

    for f in range(2):
        put(xm, f, beyond_n, recv2[2, 4 + f])
        put(xm, f, beyond_s, recv2[3, 4 + f])

    def unpack_sums(g, carry):
        at = pl.ds(pl.multiple_of(TOP + 8 * g, 8), 8)
        for f in range(4):
            put_sum(xs, f, at, beside(recv2[0, f], recv2[1, f], g))
        for f in range(2):
            put(xs, f, at, beside(recv2[0, 4 + f], recv2[1, 4 + f], g))
        return carry

    each_group(unpack_sums)

    rows = 8
    lane_r = lanes(rows)

    def around(field, here):
        main, side = xm[field, here, :], xs[field, here, :]
        e, w = shift_east(main, side, lane_r), shift_west(main, side, lane_r)
        return (xm, e[0] - w[0]), (xs, e[1] - w[1])

    def new_height(at):
        here, up, down = (slice(at + i, at + i + rows) for i in (0, 1, -1))
        for ref, across in around(EAST, here):
            spread = across + (ref[NORTH, up, :] - ref[NORTH, down, :])
            ref[HEIGHT, here, :] = ref[OCEAN, here, :] * (ref[HEIGHT, here, :] - (0.5 * COURANT) * spread)

    def new_transports(at, last):
        here, up, down = (slice(at + i, at + i + rows) for i in (0, 1, -1))
        for ref, across in around(HEIGHT, here):
            if ref is xs and last:
                continue
            old_e, old_n = ref[EAST, here, :], ref[NORTH, here, :]
            depth, f = ref[DEPTH, here, :], ref[CORIOLIS, here, :]
            ref[EAST, here, :] = (old_e + ref[F_EAST, here, :]) + (f * old_n - depth * across)
            ref[NORTH, here, :] = (old_n + ref[F_NORTH, here, :]) - (
                f * old_e + depth * (ref[HEIGHT, up, :] - ref[HEIGHT, down, :])
            )

    chunks = 144 // rows
    for stage in range(2 * SUBSTEPS):
        for i in range(chunks):
            if stage % 2 == 0:
                new_height(8 + i * rows)
            else:
                new_transports(8 + i * rows, stage == 2 * SUBSTEPS - 1)

    block = slice(TOP, TOP + N)
    floor_depth = (2.0 / COURANT) * xm[DEPTH, block, :] + (1.0 - xm[OCEAN, block, :])
    for f in range(2):
        forced = (TIMESTEP / COURANT) * xm[F_EAST + f, block, :]
        corr[f] = (xm[EAST + f, block, :] - totals[f] - forced) / floor_depth
    height_out[...] = xm[HEIGHT, block, :]
    for copy in copies.values():
        copy.wait_send()


def finish(base_e, base_n, corr, height, deep, height_h, east_h, north_h, outs, sem):
    copies = [pltpu.make_async_copy(height, height_h, sem.at[2 * LEVELS])]
    copies[0].start()
    first_level = (lax.axis_index("gz") * LEVELS).astype(jnp.float32)
    for k in range(LEVELS):
        at = pl.ds(k * N, N)
        wet = first_level + k < deep[...]
        for f, (base, target) in enumerate(((base_e, east_h), (base_n, north_h))):
            outs[f, at, :] = jnp.where(wet, base[at, :] + corr[f], 0.0)
            copy = pltpu.make_async_copy(outs.at[f, at], target.at[at], sem.at[2 * k + f])
            copy.start()
            copies.append(copy)
    for copy in copies:
        copy.wait()


def on_device(
    layer_east, layer_north, layer_press, surface, land_sea, bottom_level, coriolis, level_thick
):
    f32 = jnp.float32
    tall = (LEVELS * N, N)
    flat = (N, N)
    hbm, vmem = pl.BlockSpec(memory_space=pltpu.HBM), pl.BlockSpec(memory_space=pltpu.VMEM)
    between = pl.pallas_call(
        kernel,
        name="ocean",
        out_shape=tuple(jax.ShapeDtypeStruct(shape, f32) for shape in (tall, tall, (2, *flat), flat, flat)),
        in_specs=[hbm] * 8,
        out_specs=(vmem,) * 5,
        scratch_shapes=[
            pltpu.SMEM((LEVELS,), f32),
            *[pltpu.VMEM((LEVELS * PITCH, N), f32)] * 3,
            pltpu.VMEM((PITCH, N), f32),
            *[pltpu.VMEM(flat, f32)] * 2,
            *[pltpu.VMEM(flat, jnp.int32)] * 2,
            pltpu.VMEM((7, 8, N), f32),
            *[pltpu.VMEM((4, N, N), f32)] * 2,
            *[pltpu.VMEM((17, 8, N), f32)] * 2,
            *[pltpu.VMEM((5, 8, N), f32)] * 2,
            pltpu.VMEM((2, N, N), f32),
            *[
                pltpu.VMEM(shape, f32)
                for _ in range(2)
                for shape in ((4, 5, 8, N), (4, 6, 8, N), (4, 8, N), (4, 8, N))
            ],
            *[pltpu.VMEM((9, EXT, N), f32)] * 2,
            pltpu.SemaphoreType.DMA((29,)),
            pltpu.SemaphoreType.DMA((19,)),
            pltpu.SemaphoreType.DMA((19,)),
        ],
        compiler_params=pltpu.CompilerParams(
            collective_id=0, has_side_effects=True, vmem_limit_bytes=VMEM_LIMIT
        ),
    )(
        *(
            pltpu.with_memory_space_constraint(x, pltpu.HBM)
            for x in (
                level_thick,
                layer_east.reshape(tall),
                layer_north.reshape(tall),
                layer_press.reshape(tall),
                surface,
                land_sea,
                bottom_level,
                coriolis,
            )
        )
    )
    height, east_next, north_next = pl.pallas_call(
        finish,
        name="finish",
        out_shape=tuple(jax.ShapeDtypeStruct(shape, f32) for shape in (flat, tall, tall)),
        in_specs=[vmem] * 5,
        out_specs=(hbm,) * 3,
        scratch_shapes=[pltpu.VMEM((2, *tall), f32), pltpu.SemaphoreType.DMA((2 * LEVELS + 1,))],
        compiler_params=pltpu.CompilerParams(vmem_limit_bytes=VMEM_LIMIT),
    )(*between)
    shape = (LEVELS, N, N)
    return height, east_next.reshape(shape), north_next.reshape(shape)


def solution(mesh):
    whole, flat = P("gz", "gy", "gx"), P("gy", "gx")
    return jax.shard_map(
        on_device,
        mesh=mesh,
        in_specs=(whole, whole, whole, flat, flat, flat, flat, P("gz")),
        out_specs=(flat, whole, whole),
        check_vma=False,
    )
```

```python
import jax
import jax.numpy as jnp
from jax import lax
from jax.experimental import pallas as pl
from jax.experimental.pallas import tpu as pltpu
from jax.sharding import PartitionSpec as P

MESH = pl.DeviceIdType.MESH
SUBSTEPS = 4
COURANT = 0.25
VISCOSITY = 0.1
TIMESTEP = SUBSTEPS * COURANT
assert TIMESTEP == 1.0
VMEM_LIMIT = 16 * 2**20

N = 128
LEVELS = 8
PITCH = 144
PAD = 8
TOP = 16
EXT = 160

HEIGHT, CORIOLIS, DEEPEST, EAST, NORTH, F_EAST, F_NORTH, DEPTH, OCEAN = range(9)
TURNED = (1, 0, 3, 2)


def shift_east(main, side, lane):
    a, b = pltpu.roll(main, N - 1, 1), pltpu.roll(side, N - 1, 1)
    last = lane == N - 1
    return jnp.where(last, b, a), jnp.where(last, a, b)


def shift_west(main, side, lane):
    a, b = pltpu.roll(main, 1, 1), pltpu.roll(side, 1, 1)
    first = lane == 0
    return jnp.where(first, b, a), jnp.where(first, a, b)


def lanes(rows):
    return lax.broadcasted_iota(jnp.int32, (rows, N), 1)


def kernel(
    thick_h, east_h, north_h, press_h, surf_h, land_h, bottom_h, cor_h,
    base_e, base_n, corr, height_out, deep_out,
    thick, levels_e, levels_n, levels_p, deep, surf, cor, land, bottom,
    edges, part, part_in, swap, swap_in, late, late_in, totals,
    send1, send2, send_d1, send_d2, recv1, recv2, recv_d1, recv_d2,
    xm, xs, load_sem, send_sem, recv_sem,
):
    gx, gy, gz = lax.axis_index("gx"), lax.axis_index("gy"), lax.axis_index("gz")
    nx, ny = lax.axis_size("gx"), lax.axis_size("gy")
    east, west = lax.rem(gx + 1, nx), lax.rem(gx + nx - 1, nx)
    north, south = lax.rem(gy + 1, ny), lax.rem(gy + ny - 1, ny)
    sister = {"gz": 1 - gz}
    straight = ({"gx": east}, {"gx": west}, {"gy": north}, {"gy": south})
    diagonal = (
        {"gx": east, "gy": north}, {"gx": west, "gy": north},
        {"gx": east, "gy": south}, {"gx": west, "gy": south},
    )

    barrier = pltpu.get_barrier_semaphore()
    for other in (*diagonal, *straight, sister):
        pl.semaphore_signal(barrier, inc=1, device_id=other, device_id_type=MESH)

    loads = []

    def load(source, target):
        copy = pltpu.make_async_copy(source, target, load_sem.at[len(loads)])
        copy.start()
        loads.append(copy)

    load(thick_h, thick)
    load(land_h, land)
    load(bottom_h, bottom)
    load(surf_h, surf)
    load(cor_h, cor)
    levels = (levels_e, levels_n, levels_p)
    for source, target in zip((east_h, north_h, press_h), levels):
        for k in range(LEVELS):
            load(source.at[pl.ds(k * N, N)], target.at[pl.ds(k * PITCH + PAD, N)])

    lane = lanes(8)
    even = (lane & 1) == 0
    row = lax.broadcasted_iota(jnp.int32, (8, N), 0)
    first_level = (gz * LEVELS).astype(jnp.float32)
    zero = jnp.zeros((8, N), jnp.float32)

    def by_index(index):
        out = zero
        for k in range(LEVELS):
            out = jnp.where(index == k, thick[k], out)
        return out

    for copy in loads[:5]:
        copy.wait()
    deep[0:PAD, :] = zero
    deep[PAD + N : PITCH, :] = zero
    deepest = land[...].astype(jnp.float32) * bottom[...].astype(jnp.float32)
    deep[PAD : PAD + N, :] = deepest
    deep_out[...] = deepest

    def each_group(body, carry=()):
        def trip(i, carry):
            for u in range(4):
                carry = body(4 * i + u, carry)
            return carry

        return lax.fori_loop(0, 4, trip, carry)

    def strips(refs):
        def body(g, carry):
            to_east = (lane >> 3) == g
            to_west = (lane >> 3) == lax.rem(g + 1, 16)
            turn = lax.rem(8 * g + 8, N)
            out = []
            for i, (ref, pad) in enumerate(refs):
                v = pltpu.roll(ref[pl.ds(pl.multiple_of(g * 8 + pad, 8), 8), :], turn, 1)
                out += [jnp.where(to_east, v, carry[2 * i]), jnp.where(to_west, v, carry[2 * i + 1])]
            return tuple(out)

        tiles = each_group(body, (zero,) * (2 * len(refs)))
        return tiles[0::2], tiles[1::2]

    flat_e, flat_w = strips([(surf, 0), (cor, 0), (deep, PAD)])

    def pack_deepest(g, d_edge):
        v = pltpu.roll(deep[pl.ds(pl.multiple_of(g * 8 + PAD, 8), 8), :], 8 * g + 1, 1)
        return jnp.where(((lane - 8 * g) >> 1) == 0, v, d_edge)

    d_edge = each_group(pack_deepest, zero)
    d_edge = d_edge + pltpu.roll(d_edge, 2, 1)
    d_edge = d_edge + pltpu.roll(d_edge, 4, 1)
    edges[6] = d_edge

    edge = []
    for t, ref in enumerate(levels):
        for copy in loads[5 + LEVELS * t : 5 + LEVELS * (t + 1)]:
            copy.wait()

        def pack(g, carry, ref=ref):
            carry = list(carry)
            pair = (lane - 8 * g) >> 1
            for k in range(LEVELS):
                at = pl.multiple_of(g * 8 + (k * PITCH + PAD), 8)
                v = pltpu.roll(ref[pl.ds(at, 8), :], 8 * g + 2 * (k % 4) + 1, 1)
                carry[k // 4] = jnp.where(pair == k % 4, v, carry[k // 4])
            return tuple(carry)

        edge += each_group(pack, (zero, zero))
    for j in range(6):
        edges[j] = edge[j]
    row_n = [ref[pl.ds(PAD + N - 1, LEVELS, stride=PITCH), :] for ref in levels]
    row_s = [ref[pl.ds(PAD, LEVELS, stride=PITCH), :] for ref in levels]

    def pack_ends(tiles):
        high = low = zero
        for j, v in enumerate(tiles):
            v = pltpu.roll(v, 8 * j + 8, 1)
            high = jnp.where((lane >> 3) == j, v, high)
            low = jnp.where((lane >> 3) == j + 1, v, low)
        return high, low

    rows_e, rows_w = pack_ends([r for t in range(3) for r in (row_n[t], row_s[t])])
    cols_n, cols_s = pack_ends(edge)
    flat = (surf, cor)
    tiles_n = [ref[N - 8 : N, :] for ref in flat] + [deep[PAD + N - 8 : PAD + N, :]]
    tiles_s = [ref[0:8, :] for ref in flat] + [deep[PAD : PAD + 8, :]]
    for i, tile in enumerate((flat_e[2], flat_w[2], tiles_n[2], tiles_s[2])):
        send1[i, 0] = tile
    for t in range(3):
        a, b = edge[2 * t], edge[2 * t + 1]
        send1[0, 1 + t] = jnp.where(even, a, pltpu.roll(b, 1, 1))
        send1[1, 1 + t] = jnp.where(even, pltpu.roll(b, N - 1, 1), a)
        send1[2, 1 + t] = row_n[t]
        send1[3, 1 + t] = row_s[t]
    for i, tile in enumerate((rows_e, rows_w, cols_n, cols_s)):
        send1[i, 4] = tile
    for i, tiles in enumerate((flat_e, flat_w, tiles_n, tiles_s)):
        for f in range(2):
            send2[i, 4 + f] = tiles[f]
    ends_n = pack_ends([v for pair in zip(row_n, tiles_n) for v in pair])
    ends_s = pack_ends([v for pair in zip(row_s, tiles_s) for v in pair])
    for i, (ends, columns) in enumerate((
        (ends_n[0], cols_n), (ends_n[1], cols_n), (ends_s[0], cols_s), (ends_s[1], cols_s)
    )):
        send_d1[i] = jnp.where(lane < 64, ends, pltpu.roll(columns, 64, 1))

    swap[16] = by_index(row)

    copies = {}

    def send(name, source, target, slot, other):
        copy = pltpu.make_async_remote_copy(
            src_ref=source, dst_ref=target, send_sem=send_sem.at[slot], recv_sem=recv_sem.at[slot],
            device_id=other, device_id_type=MESH,
        )
        copy.start()
        copies[name] = copy

    def chunk(i, carry):
        rows = 8
        at = pl.multiple_of(i * rows, rows)
        lane16 = lanes(rows)
        d = deep[pl.ds(at + PAD, rows), :]
        d_e = jnp.where(lane16 == N - 1, 0.0, jnp.minimum(d, pltpu.roll(d, N - 1, 1)))
        d_w = jnp.where(lane16 == 0, 0.0, jnp.minimum(d, pltpu.roll(d, 1, 1)))
        d_n = jnp.minimum(d, deep[pl.ds(at + PAD + 1, rows), :])
        d_s = jnp.minimum(d, deep[pl.ds(at + PAD - 1, rows), :])
        f = cor[pl.ds(at, rows), :]
        sums = [jnp.zeros((rows, N), jnp.float32) for _ in range(4)]
        for k in range(LEVELS):
            level = first_level + k
            here, on_e, on_w, on_n, on_s = (level < other for other in (d, d_e, d_w, d_n, d_s))
            start = k * PITCH + PAD + at

            ve, vn, p = (ref[pl.ds(start, rows), :] for ref in levels)

            def along_y(ref, c):
                n = jnp.where(on_n, ref[pl.ds(start + 1, rows), :] - c, 0.0)
                return n, jnp.where(on_s, c - ref[pl.ds(start - 1, rows), :], 0.0)

            drag, half_p = VISCOSITY * ve, 0.5 * p
            ahead, behind = drag - half_p, drag + half_p
            x_e = jnp.where(on_e, pltpu.roll(ahead, N - 1, 1) - ahead, 0.0)
            x_w = jnp.where(on_w, behind - pltpu.roll(behind, 1, 1), 0.0)
            n_e = jnp.where(on_e, pltpu.roll(vn, N - 1, 1) - vn, 0.0)
            n_w = pltpu.roll(n_e, 1, 1)
            e_n, e_s = along_y(levels_e, ve)
            n_n, n_s = along_y(levels_n, vn)
            p_n, p_s = along_y(levels_p, p)
            masked_e = jnp.where(here, ve, 0.0)
            masked_n = jnp.where(here, vn, 0.0)
            tend_e = (x_e - x_w) + VISCOSITY * (e_n - e_s) + f * masked_n
            tend_n = VISCOSITY * ((n_e - n_w) + (n_n - n_s)) - 0.5 * (p_n + p_s) - f * masked_e
            base_e[pl.ds(k * N + at, rows), :] = masked_e + tend_e
            base_n[pl.ds(k * N + at, rows), :] = masked_n + tend_n
            weight = thick[k]
            for slot, value in enumerate((masked_e, masked_n, tend_e, tend_n)):
                sums[slot] += weight * value
        for slot in range(4):
            part[slot, pl.ds(at, rows), :] = sums[slot]
        return carry

    lax.fori_loop(0, N // 16, chunk, 0)
    pl.semaphore_wait(barrier, 9)
    for i in range(4):
        send(("d1", i), send_d1.at[i], recv_d1.at[3 - i], 3 + i, diagonal[i])
    for i in range(4):
        send(("s1", i), send1.at[i], recv1.at[TURNED[i]], 7 + i, straight[i])


    lax.fori_loop(N // 16, N // 8, chunk, 0)
    to_e, to_w = strips([(part.at[slot], 0) for slot in range(4)])
    for f in range(4):
        swap[f] = to_e[f]
        swap[4 + f] = to_w[f]
        swap[8 + f] = part[f, N - 8 : N, :]
        swap[12 + f] = part[f, 0:8, :]
    send("swap", swap, swap_in, 0, sister)

    copies["swap"].wait_recv()
    whole = [swap[j] + swap_in[j] for j in range(16)]
    for i in range(4):
        for f in range(4):
            send2[i, f] = whole[4 * i + f]
    ends_n, ends_s = pack_ends(whole[8:12]), pack_ends(whole[12:16])
    for i, tile in enumerate((*ends_n, *ends_s)):
        send_d2[i] = tile
    for i in range(4):
        send(("d2", i), send_d2.at[i], recv_d2.at[3 - i], 11 + i, diagonal[i])
    for i in range(4):
        send(("s2", i), send2.at[i], recv2.at[TURNED[i]], 15 + i, straight[i])
    send("part", part, part_in, 1, sister)

    upper = gz == 1
    own_thick, other_thick = 0.5 * COURANT * swap[16], 0.5 * COURANT * swap_in[16]
    thick_low = jnp.where(upper, other_thick, own_thick)
    thick_high = jnp.where(upper, own_thick, other_thick)

    def depth_of(d):
        out = jnp.zeros_like(d)
        for k in range(2 * LEVELS):
            tile = thick_low if k < LEVELS else thick_high
            weight = jnp.broadcast_to(tile[k % LEVELS : k % LEVELS + 1, :], d.shape)
            out = out + jnp.where(k < d, weight, 0.0)
        return out

    def settle(ref, at, rows):
        d = ref[DEEPEST, pl.ds(at, rows), :]
        ref[DEPTH, pl.ds(at, rows), :] = depth_of(d)
        ref[OCEAN, pl.ds(at, rows), :] = jnp.where(d > 0.0, 1.0, 0.0)

    xm[HEIGHT, TOP : TOP + N, :] = surf[...]
    xm[CORIOLIS, TOP : TOP + N, :] = COURANT * cor[...]
    xm[DEEPEST, TOP : TOP + N, :] = deep[PAD : PAD + N, :]

    def settle_main(i, carry):
        settle(xm, pl.multiple_of(TOP + 32 * i, 8), 32)
        return carry

    lax.fori_loop(0, N // 32, settle_main, 0)
    for i in range(4):
        copies["d1", i].wait_recv()
        copies["s1", i].wait_recv()
    from_e, from_w, from_n, from_s = (recv1.at[i] for i in range(4))

    def beside(tile_e, tile_w, index):
        following = lax.rem(index + 1, 16)
        both = jnp.where((lane >> 3) == following, tile_e, tile_w)
        return pltpu.roll(both, lax.rem(N - 8 * following, N), 1)

    def put(ref, f, at, tile):
        ref[f, at, :] = COURANT * tile if f in (CORIOLIS, F_EAST, F_NORTH) else tile

    beyond_n, beyond_s = pl.ds(TOP + N, 8), pl.ds(TOP - 8, 8)
    corners = [recv_d1[i] for i in range(4)]
    d_north = beside(corners[0], corners[1], 5)
    d_south = beside(corners[2], corners[3], 5)
    d_first, d_last = (beside(from_e[0], from_w[0], g) for g in (0, 15))

    east_of = lane & 1
    sign = jnp.where(even, -0.5, 0.5)
    in_group = lane & 7

    strip_d = jnp.where(
        in_group == 0, pltpu.roll(from_e[0], N - 8, 1),
        jnp.where(in_group == 1, pltpu.roll(from_w[0], N - 6, 1), 0.0),
    )
    strip_d = strip_d + pltpu.roll(strip_d, 2, 1)
    strip_d = strip_d + pltpu.roll(strip_d, 4, 1)
    own_d = edges[6]
    column_terms = []
    sums_g = sums_e = sums_n = zero
    for half in range(2):
        level_in = (in_group >> 1) + 4 * half
        level = level_in.astype(jnp.float32) + first_level
        both = (level < own_d) & (level < strip_d)
        weight = by_index(level_in)
        diff = []
        for t in range(3):
            if half == 0:
                halo = jnp.where(even, pltpu.roll(from_e[1 + t], N - 1, 1), pltpu.roll(from_w[1 + t], 1, 1))
            else:
                halo = jnp.where(even, from_e[1 + t], from_w[1 + t])
            diff.append(jnp.where(both, halo - edges[2 * t + half], 0.0))
        drag_e, drag_n, grad = VISCOSITY * diff[0], VISCOSITY * diff[1], sign * diff[2]
        column_terms.append((grad + drag_e, drag_n))
        sums_g = sums_g + weight * grad
        sums_e = sums_e + weight * drag_e
        sums_n = sums_n + weight * drag_n

    def over_levels(v):
        v = v + pltpu.roll(v, N - 2, 1)
        return v + pltpu.roll(v, N - 4, 1)

    def swapped(v):
        return jnp.where(even, pltpu.roll(v, N - 1, 1), pltpu.roll(v, 1, 1))

    sums_g, sums_e, sums_n = over_levels(sums_g), over_levels(sums_e), over_levels(sums_n)
    late[0] = jnp.where(
        in_group < 2, sums_g + sums_e,
        jnp.where(
            in_group < 4, pltpu.roll(sums_n, 2, 1),
            jnp.where(
                in_group < 6, pltpu.roll(swapped(sums_g - sums_e), 4, 1), pltpu.roll(swapped(-sums_n), 6, 1)
            ),
        ),
    )

    in_tile = (lane & 15) >> 1
    tile_level = in_tile.astype(jnp.float32) + first_level
    tile_weight = by_index(in_tile) * jnp.where(lane < 32, VISCOSITY, sign)
    for slot, (tile, ahead, behind, side, near, far) in enumerate((
        (from_n[4], corners[0], corners[1], d_north, from_n[0], N - 8),
        (from_s[4], corners[2], corners[3], d_south, from_s[0], 0),
    )):

        def ends(v, a, b):
            return jnp.where(
                even, jnp.broadcast_to(v[:, a : a + 1], (8, N)), jnp.broadcast_to(v[:, b : b + 1], (8, N))
            )

        both = (tile_level < ends(near, N - 1, 0)) & (tile_level < ends(side, 0, N - 1))
        halo = jnp.where(even, pltpu.roll(ahead, 63, 1), pltpu.roll(behind, 65, 1))
        diff = halo - tile
        if far:
            diff = pltpu.roll(diff, far, 1)
        v = over_levels(jnp.where(both, tile_weight * diff, 0.0))
        late[1 + slot] = v + pltpu.roll(v, N - 8, 1)

    row_level = row.astype(jnp.float32) + first_level
    row_weight = by_index(row)

    def row_pairs(own, halo, d_own, d_halo, factor):
        both = (row_level < d_own) & (row_level < d_halo)
        diff = [jnp.where(both, h - o, 0.0) for h, o in zip(halo, own)]
        return factor * diff[2], VISCOSITY * diff[0], VISCOSITY * diff[1]

    def spread_row(v):
        return jnp.broadcast_to(v, (8, N))

    own_rows_n = [ref[pl.ds(PAD + N - 1, LEVELS, stride=PITCH), :] for ref in levels]
    own_rows_s = [ref[pl.ds(PAD, LEVELS, stride=PITCH), :] for ref in levels]
    main_n = row_pairs(
        own_rows_n, [from_n[1 + t] for t in range(3)],
        spread_row(deep[PAD + N - 1 : PAD + N, :]), spread_row(from_n[0, 0:1, :]), -0.5,
    )
    main_s = row_pairs(
        own_rows_s, [from_s[1 + t] for t in range(3)],
        spread_row(deep[PAD : PAD + 1, :]), spread_row(from_s[0, 7:8, :]), 0.5,
    )
    side_n = row_pairs(
        [beside(from_e[4], from_w[4], 2 * t) for t in range(3)],
        [beside(corners[0], corners[1], 2 * t) for t in range(3)],
        spread_row(d_last[7:8, :]), spread_row(d_north[0:1, :]), -0.5,
    )
    side_s = row_pairs(
        [beside(from_e[4], from_w[4], 2 * t + 1) for t in range(3)],
        [beside(corners[2], corners[3], 2 * t) for t in range(3)],
        spread_row(d_first[0:1, :]), spread_row(d_south[7:8, :]), 0.5,
    )
    for slot, pairs in ((3, (main_n, main_s)), (4, (side_n, side_s))):
        tile = zero
        for i, terms in enumerate(pairs):
            for j, term in enumerate(terms):
                total = jnp.sum(row_weight * term, axis=0, keepdims=True)
                tile = jnp.where(row == 3 * i + j, spread_row(total), tile)
        late[slot] = tile
    send("late", late, late_in, 2, sister)

    for at, (grad, drag_e, drag_n) in ((N - 1, main_n), (0, main_s)):
        where_ = pl.ds(at, LEVELS, stride=N)
        base_e[where_, :] = base_e[where_, :] + drag_e
        base_n[where_, :] = base_n[where_, :] + (grad + drag_n)
    for half in range(2):
        for j in range(2):
            edges[2 * half + j] = column_terms[half][j]
    outer = (lane == 0) | (lane == N - 1)

    def add_columns(g, carry):
        for k in range(LEVELS):
            at = pl.multiple_of(g * 8 + k * N, 8)
            turn = (N - 1 - 2 * (k % 4)) - 8 * g
            for j, ref in enumerate((base_e, base_n)):
                v = pltpu.roll(edges[2 * (k // 4) + j], turn, 1)
                ref[pl.ds(at, 8), :] = ref[pl.ds(at, 8), :] + jnp.where(outer, v, 0.0)
        return carry

    put(xm, DEEPEST, beyond_n, from_n[0])
    put(xm, DEEPEST, beyond_s, from_s[0])
    for f in range(3):
        put(xs, f, beyond_n, beside(corners[0], corners[1], 2 * f + 1))
        put(xs, f, beyond_s, beside(corners[2], corners[3], 2 * f + 1))

    def unpack_deepest(g, carry):
        put(xs, DEEPEST, pl.ds(pl.multiple_of(TOP + 8 * g, 8), 8), beside(from_e[0], from_w[0], g))
        return carry

    each_group(unpack_deepest)
    each_group(add_columns)

    def settle_side(i, carry):
        settle(xs, pl.multiple_of(8 + 48 * i, 8), 48)
        return carry

    lax.fori_loop(0, 3, settle_side, 0)
    settle(xm, TOP - 8, 8)
    settle(xm, TOP + N, 8)

    def add_to(ref, field, at, value):
        ref[field, at, :] = ref[field, at, :] + value

    copies["part"].wait_recv()
    for f in range(4):
        whole_f = part[f] + part_in[f]
        xm[EAST + f, TOP : TOP + N, :] = whole_f if f < 2 else COURANT * whole_f
        if f < 2:
            totals[f] = whole_f
    copies["late"].wait_recv()
    column_sum = COURANT * (late[0] + late_in[0])

    def place_columns(g, carry):
        at = pl.ds(pl.multiple_of(TOP + 8 * g, 8), 8)
        for f in range(2):
            turn = (N - 1 - 2 * f) - 8 * g
            add_to(xm, F_EAST + f, at, jnp.where(outer, pltpu.roll(column_sum, turn, 1), 0.0))
            xs[F_EAST + f, at, :] = jnp.where(outer, pltpu.roll(column_sum, turn - 4, 1), 0.0)
        return carry

    each_group(place_columns)
    for slot, at in ((1, beyond_n), (2, beyond_s)):
        v = COURANT * (late[slot] + late_in[slot])
        drag_e, drag_n, grad = v, pltpu.roll(v, N - 16, 1), pltpu.roll(v, N - 32, 1)
        xm[F_EAST, at, :] = jnp.where(outer, pltpu.roll(grad + drag_e, N - 1, 1), 0.0)
        xm[F_NORTH, at, :] = jnp.where(outer, pltpu.roll(drag_n, N - 1, 1), 0.0)
        xs[F_EAST, at, :] = jnp.where(outer, pltpu.roll(swapped(grad - drag_e), N - 1, 1), 0.0)
        xs[F_NORTH, at, :] = jnp.where(outer, pltpu.roll(swapped(-drag_n), N - 1, 1), 0.0)
    for slot, ref in ((3, xm), (4, xs)):
        v = COURANT * (late[slot] + late_in[slot])
        for i, (own, halo) in enumerate(((TOP + N - 1, TOP + N), (TOP, TOP - 1))):
            grad, drag_e, drag_n = (v[3 * i + j : 3 * i + j + 1, :] for j in range(3))
            add_to(ref, F_EAST, pl.ds(own, 1), drag_e)
            add_to(ref, F_NORTH, pl.ds(own, 1), grad + drag_n)
            add_to(ref, F_EAST, pl.ds(halo, 1), -drag_e)
            add_to(ref, F_NORTH, pl.ds(halo, 1), grad - drag_n)

    for i in range(4):
        copies["d2", i].wait_recv()
        copies["s2", i].wait_recv()

    def put_sum(ref, f, at, tile):
        if f < 2:
            ref[EAST + f, at, :] = tile
        else:
            add_to(ref, EAST + f, at, COURANT * tile)

    for f in range(4):
        put_sum(xm, f, beyond_n, recv2[2, f])
        put_sum(xm, f, beyond_s, recv2[3, f])
        put_sum(xs, f, beyond_n, beside(recv_d2[0], recv_d2[1], f))
        put_sum(xs, f, beyond_s, beside(recv_d2[2], recv_d2[3], f))

    for f in range(2):
        put(xm, f, beyond_n, recv2[2, 4 + f])
        put(xm, f, beyond_s, recv2[3, 4 + f])

    def unpack_sums(g, carry):
        at = pl.ds(pl.multiple_of(TOP + 8 * g, 8), 8)
        for f in range(4):
            put_sum(xs, f, at, beside(recv2[0, f], recv2[1, f], g))
        for f in range(2):
            put(xs, f, at, beside(recv2[0, 4 + f], recv2[1, 4 + f], g))
        return carry

    each_group(unpack_sums)

    rows = 8
    lane_r = lanes(rows)

    def around(field, here):
        main, side = xm[field, here, :], xs[field, here, :]
        e, w = shift_east(main, side, lane_r), shift_west(main, side, lane_r)
        return (xm, e[0] - w[0]), (xs, e[1] - w[1])

    def new_height(at):
        here, up, down = (slice(at + i, at + i + rows) for i in (0, 1, -1))
        for ref, across in around(EAST, here):
            spread = across + (ref[NORTH, up, :] - ref[NORTH, down, :])
            ref[HEIGHT, here, :] = ref[OCEAN, here, :] * (ref[HEIGHT, here, :] - (0.5 * COURANT) * spread)

    def new_transports(at, last):
        here, up, down = (slice(at + i, at + i + rows) for i in (0, 1, -1))
        for ref, across in around(HEIGHT, here):
            if ref is xs and last:
                continue
            old_e, old_n = ref[EAST, here, :], ref[NORTH, here, :]
            depth, f = ref[DEPTH, here, :], ref[CORIOLIS, here, :]
            ref[EAST, here, :] = (old_e + ref[F_EAST, here, :]) + (f * old_n - depth * across)
            ref[NORTH, here, :] = (old_n + ref[F_NORTH, here, :]) - (
                f * old_e + depth * (ref[HEIGHT, up, :] - ref[HEIGHT, down, :])
            )

    chunks = 144 // rows
    for stage in range(2 * SUBSTEPS):
        for i in range(chunks):
            if stage % 2 == 0:
                new_height(8 + i * rows)
            else:
                new_transports(8 + i * rows, stage == 2 * SUBSTEPS - 1)

    block = slice(TOP, TOP + N)
    floor_depth = (2.0 / COURANT) * xm[DEPTH, block, :] + (1.0 - xm[OCEAN, block, :])
    for f in range(2):
        forced = (TIMESTEP / COURANT) * xm[F_EAST + f, block, :]
        corr[f] = (xm[EAST + f, block, :] - totals[f] - forced) / floor_depth
    height_out[...] = xm[HEIGHT, block, :]
    for copy in copies.values():
        copy.wait_send()


def finish(base_e, base_n, corr, height, deep, height_h, east_h, north_h, outs, sem):
    copies = [pltpu.make_async_copy(height, height_h, sem.at[2 * LEVELS])]
    copies[0].start()
    first_level = (lax.axis_index("gz") * LEVELS).astype(jnp.float32)
    for k in range(LEVELS):
        at = pl.ds(k * N, N)
        wet = first_level + k < deep[...]
        for f, (base, target) in enumerate(((base_e, east_h), (base_n, north_h))):
            outs[f, at, :] = jnp.where(wet, base[at, :] + corr[f], 0.0)
            copy = pltpu.make_async_copy(outs.at[f, at], target.at[at], sem.at[2 * k + f])
            copy.start()
            copies.append(copy)
    for copy in copies:
        copy.wait()


def on_device(
    layer_east, layer_north, layer_press, surface, land_sea, bottom_level, coriolis, level_thick
):
    f32 = jnp.float32
    tall = (LEVELS * N, N)
    flat = (N, N)
    hbm, vmem = pl.BlockSpec(memory_space=pltpu.HBM), pl.BlockSpec(memory_space=pltpu.VMEM)
    between = pl.pallas_call(
        kernel,
        name="ocean",
        out_shape=tuple(jax.ShapeDtypeStruct(shape, f32) for shape in (tall, tall, (2, *flat), flat, flat)),
        in_specs=[hbm] * 8,
        out_specs=(vmem,) * 5,
        scratch_shapes=[
            pltpu.SMEM((LEVELS,), f32),
            *[pltpu.VMEM((LEVELS * PITCH, N), f32)] * 3,
            pltpu.VMEM((PITCH, N), f32),
            *[pltpu.VMEM(flat, f32)] * 2,
            *[pltpu.VMEM(flat, jnp.int32)] * 2,
            pltpu.VMEM((7, 8, N), f32),
            *[pltpu.VMEM((4, N, N), f32)] * 2,
            *[pltpu.VMEM((17, 8, N), f32)] * 2,
            *[pltpu.VMEM((5, 8, N), f32)] * 2,
            pltpu.VMEM((2, N, N), f32),
            *[
                pltpu.VMEM(shape, f32)
                for _ in range(2)
                for shape in ((4, 5, 8, N), (4, 6, 8, N), (4, 8, N), (4, 8, N))
            ],
            *[pltpu.VMEM((9, EXT, N), f32)] * 2,
            pltpu.SemaphoreType.DMA((29,)),
            pltpu.SemaphoreType.DMA((19,)),
            pltpu.SemaphoreType.DMA((19,)),
        ],
        compiler_params=pltpu.CompilerParams(
            collective_id=0, has_side_effects=True, vmem_limit_bytes=VMEM_LIMIT
        ),
    )(
        *(
            pltpu.with_memory_space_constraint(x, pltpu.HBM)
            for x in (
                level_thick,
                layer_east.reshape(tall),
                layer_north.reshape(tall),
                layer_press.reshape(tall),
                surface,
                land_sea,
                bottom_level,
                coriolis,
            )
        )
    )
    height, east_next, north_next = pl.pallas_call(
        finish,
        name="finish",
        out_shape=tuple(jax.ShapeDtypeStruct(shape, f32) for shape in (flat, tall, tall)),
        in_specs=[vmem] * 5,
        out_specs=(hbm,) * 3,
        scratch_shapes=[pltpu.VMEM((2, *tall), f32), pltpu.SemaphoreType.DMA((2 * LEVELS + 1,))],
        compiler_params=pltpu.CompilerParams(vmem_limit_bytes=VMEM_LIMIT),
    )(*between)
    shape = (LEVELS, N, N)
    return height, east_next.reshape(shape), north_next.reshape(shape)


def solution(mesh):
    whole, flat = P("gz", "gy", "gx"), P("gy", "gx")
    return jax.shard_map(
        on_device,
        mesh=mesh,
        in_specs=(whole, whole, whole, flat, flat, flat, flat, P("gz")),
        out_specs=(flat, whole, whole),
        check_vma=False,
    )
```
